128 devices in a mesh: occ: 4 (over x_lo, core), vir: 32 (over x_hi, y, z).
Axes of the slice: x: 4 (x_hi: 2, x_lo: 2; x = x_hi * 2 + x_lo), y: 4, z: 4, core: 2. Of those that a mesh axis runs over, the one named last changes fastest.
Arguments:
- amplitudes: bfloat16 [64, 2400, 2400], P('occ', 'vir'), as said below
- integrals: bfloat16 [64, 2400, 2400], P('occ', 'vir'), may hold values from -6 to 6
- fock_vv: bfloat16 [2400, 2400], replicated, may hold values from -0.125 to 0.125
- eps_occ: float32 [240], replicated, may hold values from -2 to -0.5
- eps_vir: float32 [2400], replicated, may hold values from 0.3 to 3
- pair_ids: int32 [64, 2], P('occ'), may hold values from 0 to 239, as said below
- mirror_row: int32 [64], P('occ'), may hold values from 0 to 15, as said below
Outputs:
- updated: float32 [64, 2400, 2400], P('occ', 'vir')
The draws below stay inside these ranges and needn't reach their ends.
Inputs may be any that keep to these rules, and one draw needn't show every extreme that they name: `pair_ids`: each row's mirror pair (j, i) lies in the block of 16 rows whose index differs in the lowest bit, at row mirror_row; mirroring twice returns the row; i differs from j. `mirror_row`: within each block a permutation of the rows; the map of the partner block is its inverse. The amplitudes of a mirror pair are the amplitudes of the pair with the two virtual indices exchanged.
All inputs are finite; a program needn't handle non-finite values.
Results may differ from the reference program's by a relative error of at most 0.0029.
Values may be sent and summed in bfloat16 or wider, within the bound.
No kernel may reach another device: no remote copies, remote signals or barrier semaphores. Data moves between devices by JAX's collectives and lax.ppermute only.
A program may use at most 192 MiB of HBM per device.

```python
import jax
import jax.numpy as jnp
from jax import lax

OCC = 240
VIR = 2400
PAIR_DEV = 16
PAIRS = 64


def mirror_perms(key):
    halves = PAIRS // PAIR_DEV // 2
    keys = jax.random.split(jax.random.fold_in(key, 101), halves)
    perms = jax.vmap(lambda single: jax.random.permutation(single, PAIR_DEV))(keys).astype(jnp.int32)
    return (perms, jnp.argsort(perms, axis=1).astype(jnp.int32))


def draw_mirror_row(key, part):
    perms, inverse = mirror_perms(key)
    return jnp.stack([perms, inverse], axis=1).reshape(PAIRS).astype(jnp.int32)


def draw_pair_ids(key, part):
    perms, inverse = mirror_perms(key)
    halves = PAIRS // PAIR_DEV // 2
    key_one = jax.random.fold_in(key, 202)
    key_two = jax.random.fold_in(key, 203)
    first = jax.random.randint(key_one, (halves, PAIR_DEV), 0, OCC).astype(jnp.int32)
    step = jax.random.randint(key_two, (halves, PAIR_DEV), 1, OCC).astype(jnp.int32)
    second = (first + step) % OCC
    first = first.at[0, 0].set(OCC - 1)
    second = second.at[0, 0].set(0)
    even = jnp.stack([first, second], axis=-1)
    swapped = jnp.stack([second, first], axis=-1)
    odd = jax.vmap(lambda table, order: table[order])(swapped, inverse)
    return jnp.stack([even, odd], axis=1).reshape(PAIRS, 2).astype(jnp.int32)


def draw_amplitudes(key, part):
    perms, inverse = mirror_perms(key)
    halves = PAIRS // PAIR_DEV // 2
    key_one = jax.random.fold_in(key, 303)
    base = jax.random.normal(key_one, (halves, PAIR_DEV, VIR, VIR), jnp.float32)
    swapped = jnp.swapaxes(base, 2, 3)
    odd = jax.vmap(lambda table, order: table[order])(swapped, inverse)
    return jnp.stack([base, odd], axis=1).reshape(PAIRS, VIR, VIR).astype(jnp.bfloat16)


def level_of(own_key, dims, shards, smallest, largest):
    def one(position, shards_of):
        draws = jax.random.uniform(jax.random.fold_in(jax.random.fold_in(own_key, 6), position), (shards_of,), jnp.float32, smallest / len(shards), largest / len(shards))
        return jnp.repeat(jnp.exp(draws), dims[position] // shards_of).reshape((-1,) + (1,) * (len(dims) - position - 1))

    gain = one(*shards[0])
    for cut in shards[1:]:
        gain = gain * one(*cut)
    return gain


def centred(rng, dims, deviation, bound, shards=(), kind=jnp.bfloat16):
    level = level_of(rng, dims, shards, -0.22, 0.18) if shards else 1.0
    drawn = jax.random.normal(rng, dims, jnp.float32) * deviation * level
    return jnp.minimum(jnp.maximum(drawn, -bound), bound).astype(kind)


def setup_inputs(seed: int = 0) -> dict:
    seeds = jax.random.split(jax.random.key(seed), 8)
    return {
        "amplitudes": draw_amplitudes(jax.random.fold_in(seeds[7], 71), 0),
        "integrals": centred(seeds[1], (PAIRS, VIR, VIR), 1.0, 6.0, ((0, 4), (1, 32))),
        "fock_vv": centred(seeds[2], (VIR, VIR), VIR ** -0.5, 0.125),
        "eps_occ": jnp.clip(jax.random.uniform(seeds[3], (OCC,), jnp.float32, -2.0, -0.5), -2.0, -0.5),
        "eps_vir": jnp.clip(jax.random.uniform(seeds[4], (VIR,), jnp.float32, 0.3, 3.0), 0.3, 3.0),
        "pair_ids": draw_pair_ids(jax.random.fold_in(seeds[7], 71), 0),
        "mirror_row": draw_mirror_row(jax.random.fold_in(seeds[7], 71), 0),
    }


def reference(amplitudes, integrals, fock_vv, eps_occ, eps_vir, pair_ids, mirror_row):
    rows = jnp.arange(PAIRS, dtype=jnp.int32)
    block = rows // PAIR_DEV
    partner = block + 1 - 2 * (block % 2)
    mirror = (partner * PAIR_DEV + mirror_row).astype(jnp.int32)

    def one_pair(index):
        own = amplitudes[index]
        other = amplitudes[mirror[index]]
        tilde = (2.0 * own.astype(jnp.float32) - other.astype(jnp.float32)).astype(jnp.bfloat16)
        right_term = jnp.dot(tilde, fock_vv.T, preferred_element_type=jnp.float32).astype(jnp.bfloat16)
        left_term = jnp.dot(fock_vv, tilde, preferred_element_type=jnp.float32).astype(jnp.bfloat16)
        first = pair_ids[index, 0]
        second = pair_ids[index, 1]
        denom = eps_occ[first] + eps_occ[second] - eps_vir[:, None] - eps_vir[None, :]
        total = integrals[index].astype(jnp.float32) + right_term.astype(jnp.float32) + left_term.astype(jnp.float32)
        return own.astype(jnp.float32) + total / denom

    return lax.map(one_pair, rows)
```

```python
import functools

import jax
import jax.numpy as jnp
from jax import lax
from jax.experimental import pallas as pl
from jax.experimental.pallas import tpu as pltpu
from jax.sharding import PartitionSpec as P

BF = jnp.bfloat16
F32 = jnp.float32
LANE = 128
HI = 5
LO = (8, 7)
STEP_V = 8


def nt(a, b):
    return lax.dot_general(a, b, (((1,), (1,)), ((), ())), preferred_element_type=F32)


def params(mib, *semantics):
    return pltpu.CompilerParams(
        vmem_limit_bytes=mib << 20, dimension_semantics=semantics or ("arbitrary",)
    )


def cost(flops, moved):
    return pl.CostEstimate(flops=int(flops), bytes_accessed=int(moved), transcendentals=0)


def fprep_kernel(width, f_ref, one_ref, two_ref):
    span = STEP_V * width
    row = lax.broadcasted_iota(jnp.int32, (STEP_V * HI * 8, 1), 0)
    dest, hi, lo = row // (HI * 8), (row // 8) % HI, row % 8
    for part in range(2):
        start = part * span // 16 * 16
        size = -(-((part + 1) * span - start) // 16) * 16
        window = f_ref[start : start + size, :]
        col = lax.broadcasted_iota(jnp.int32, (1, size), 1) + start - part * span
        for chunk, out in enumerate((one_ref, two_ref)):
            base = sum(LO[:chunk]) * HI
            source = jnp.where(lo < LO[chunk], dest * width + base + lo * HI + hi, -1000)
            hot = (source == col).astype(F32).astype(BF)
            rows = STEP_V * HI * 8
            out[part * rows : (part + 1) * rows, :] = jnp.dot(
                hot, window, preferred_element_type=F32
            ).astype(BF)


def fprep(fock, count):
    vir = fock.shape[0]
    width = vir // count
    steps = count // (2 * STEP_V)
    rows = 2 * STEP_V * HI * 8
    out = jax.ShapeDtypeStruct((count * HI * 8, vir), BF)
    return pl.pallas_call(
        functools.partial(fprep_kernel, width),
        grid=(steps,),
        in_specs=[pl.BlockSpec((2 * STEP_V * width, vir), lambda i: (i, 0))],
        out_specs=[pl.BlockSpec((rows, vir), lambda i: (i, 0))] * 2,
        out_shape=[out, out],
        compiler_params=params(48),
        cost_estimate=cost(2e9, 24e6),
        name="fock_rows",
    )(fock)


def xprep_kernel(width, pick_ref, move_ref, own_ref, other_ref, out_ref):
    pairs, vir = own_ref.shape[1], own_ref.shape[2]
    left = (width - pl.program_id(0) * 16) * pairs
    row = lax.broadcasted_iota(jnp.int32, (16 * pairs, 1), 0)
    zero = jnp.zeros((), F32)
    own = own_ref[...].reshape(16 * pairs, vir)
    other = other_ref[...].reshape(16 * pairs, vir)
    own = jnp.where(row < left, own.astype(F32), zero).astype(BF)
    other = jnp.where(row < left, other.astype(F32), zero).astype(BF)
    mine = jnp.dot(move_ref[...], own, preferred_element_type=F32)
    theirs = jnp.dot(pick_ref[...], other, preferred_element_type=F32)
    out_ref[...] = (2.0 * theirs - mine).astype(BF).reshape(pairs, 16, vir)


def xprep(pick, move, own, other):
    width, pairs, vir = own.shape
    steps = -(-width // 16)
    block = pl.BlockSpec((16, pairs, vir), lambda j: (j, 0, 0))
    fixed = pl.BlockSpec((16 * pairs, 16 * pairs), lambda j: (0, 0))
    return pl.pallas_call(
        functools.partial(xprep_kernel, width),
        grid=(steps,),
        in_specs=[fixed, fixed, block, block],
        out_specs=pl.BlockSpec((pairs, 16, vir), lambda j: (0, j, 0)),
        out_shape=jax.ShapeDtypeStruct((pairs, 16 * steps, vir), BF),
        compiler_params=params(48),
        cost_estimate=cost(3e9, 18e6),
        name="tilde_mirror",
    )(pick, move, own, other)


def send_kernel(width, lo_count, f_ref, x_ref, out_ref, acc_ref, wire_ref):
    pairs, pitch, vir = x_ref.shape
    lanes = pairs * pitch
    x2 = x_ref.reshape(lanes, vir)
    for n in range(0, lanes, 256):
        acc_ref[:, n : n + 256] = nt(f_ref[...], x2[n : n + 256, :])
    lane = lax.broadcasted_iota(jnp.int32, (8, LANE), 1)
    tiles = out_ref.shape[2] // LANE

    def one(v, carry):
        row = pl.multiple_of(v * (HI * 8), 8)
        for p in range(pairs):
            tile, off = divmod(p * pitch, LANE)
            into = [None] * tiles
            for h in range(HI):
                rows = pl.ds(pl.multiple_of(row + 8 * h, 8), 8)
                seg = acc_ref[rows, tile * LANE : (tile + 1) * LANE]
                if off + width > LANE:
                    nxt = acc_ref[rows, (tile + 1) * LANE : (tile + 2) * LANE]
                    seg = jnp.where(lane >= off, seg, nxt)
                to, at = divmod(h * width, LANE)
                shift = (at - off) % LANE
                if shift:
                    seg = pltpu.roll(seg, shift, 1)
                into[to] = seg if into[to] is None else jnp.where(lane >= at, seg, into[to])
                if at + width > LANE:
                    into[to + 1] = seg
            for t in range(tiles):
                wire_ref[t, pl.ds(p, 8, stride=pairs), :] = into[t]
        for t in range(tiles):
            block = wire_ref[t, : lo_count * pairs, :].astype(BF)
            out_ref[v, :, t * LANE : (t + 1) * LANE] = block
        return carry

    lax.fori_loop(0, out_ref.shape[0], one, 0)


def send(fock_rows, x, count, width, lo_count):
    pairs, pitch, vir = x.shape
    rows = STEP_V * HI * 8
    wide = -(-HI * width // LANE) * LANE
    return pl.pallas_call(
        functools.partial(send_kernel, width, lo_count),
        grid=(count // STEP_V,),
        in_specs=[
            pl.BlockSpec((rows, vir), lambda i: (i, 0)),
            pl.BlockSpec((pairs, pitch, vir), lambda i: (0, 0, 0)),
        ],
        out_specs=pl.BlockSpec((STEP_V, lo_count * pairs, wide), lambda i: (i, 0, 0)),
        out_shape=jax.ShapeDtypeStruct((count, lo_count * pairs, wide), BF),
        scratch_shapes=[
            pltpu.VMEM((rows, pairs * pitch), F32),
            pltpu.VMEM((wide // LANE, 8 * pairs, LANE), F32),
        ],
        compiler_params=params(48),
        cost_estimate=cost(2.0 * count * HI * 8 * pairs * pitch * vir, 16e6),
        name="left_send",
    )(fock_rows, x)


def right_kernel(swap_ref, own_ref, other_ref, int_ref, f_ref, row_ref, vir_ref, out_ref):
    part, pairs, vir = own_ref.shape
    rows = part * pairs
    own = own_ref[...].reshape(rows, vir)
    other = other_ref[...].reshape(rows, vir)
    theirs = jnp.dot(swap_ref[...], other, preferred_element_type=F32)
    tilde = (2.0 * own.astype(F32) - theirs).astype(BF)
    for n in range(0, vir, 512):
        m = min(n + 512, vir)
        right = nt(tilde, f_ref[n:m, :]).astype(BF).astype(F32)
        denom = row_ref[...].reshape(rows, 1) - vir_ref[:, n:m]
        total = int_ref[:, :, n:m].reshape(rows, m - n).astype(F32) + right
        res = own_ref[:, :, n:m].reshape(rows, m - n).astype(F32) + total / denom
        out_ref[:, :, n:m] = res.reshape(part, pairs, m - n)


def right(swap, own, other, integrals, fock, rowterm, vir_row, part=15):
    width, pairs, vir = own.shape
    block = pl.BlockSpec((part, pairs, vir), lambda j: (j, 0, 0))
    return pl.pallas_call(
        right_kernel,
        grid=(width // part,),
        in_specs=[
            pl.BlockSpec((part * pairs, part * pairs), lambda j: (0, 0)),
            block,
            block,
            block,
            pl.BlockSpec((vir, vir), lambda j: (0, 0)),
            pl.BlockSpec((part, pairs, 1), lambda j: (j, 0, 0)),
            pl.BlockSpec((1, vir), lambda j: (0, 0)),
        ],
        out_specs=block,
        out_shape=jax.ShapeDtypeStruct((width, pairs, vir), F32),
        compiler_params=params(56),
        cost_estimate=cost(2.0 * width * pairs * vir * vir, 40e6),
        name="right_term",
    )(swap, own, other, integrals, fock, rowterm, vir_row)


def finish_kernel(width, got_ref, row_ref, vir_ref, base_ref, out_ref):
    count = got_ref.shape[0]
    pairs, vir = base_ref.shape[1], base_ref.shape[2]
    lane = lax.broadcasted_iota(jnp.int32, (pairs, LANE), 1)
    tiles = -(-vir // LANE)
    for h in range(HI):
        src, off = divmod(h * width, LANE)
        into = [None] * (tiles + 1)
        denom = row_ref[h]
        for w in range(count):
            seg = got_ref[w, :, src * LANE : (src + 1) * LANE].astype(F32)
            if off + width > LANE:
                nxt = got_ref[w, :, (src + 1) * LANE : (src + 2) * LANE].astype(F32)
                seg = jnp.where(lane >= off, seg, nxt)
            to, at = divmod(w * width, LANE)
            shift = (at - off) % LANE
            if shift:
                seg = pltpu.roll(seg, shift, 1)
            into[to] = seg if into[to] is None else jnp.where(lane >= at, seg, into[to])
            if at + width > LANE:
                into[to + 1] = seg
            if at + width >= LANE or w == count - 1:
                a, b = to * LANE, min((to + 1) * LANE, vir)
                value = into[to][:, : b - a] / (denom - vir_ref[:, a:b])
                out_ref[h, :, a:b] = base_ref[h, :, a:b] + value
                if w == count - 1 and at + width > LANE:
                    a, b = b, vir
                    value = into[to + 1][:, : b - a] / (denom - vir_ref[:, a:b])
                    out_ref[h, :, a:b] = base_ref[h, :, a:b] + value


def finish(got, rowterm, vir_row, base, lo_count, skip):
    count, _, wide = got.shape
    width, pairs, vir = base.shape
    block = pl.BlockSpec((HI, pairs, vir), lambda j: (j + skip, 0, 0))
    return pl.pallas_call(
        functools.partial(finish_kernel, width),
        grid=(lo_count,),
        in_specs=[
            pl.BlockSpec((count, pairs, wide), lambda j: (0, j, 0)),
            pl.BlockSpec((HI, pairs, 1), lambda j: (j + skip, 0, 0)),
            pl.BlockSpec((1, vir), lambda j: (0, 0)),
            block,
        ],
        out_specs=block,
        out_shape=jax.ShapeDtypeStruct((width, pairs, vir), F32),
        input_output_aliases={3: 0},
        compiler_params=params(32),
        cost_estimate=cost(1e8, 16e6),
        name="left_add",
    )(got, rowterm, vir_row, base)


def one_hot(target, size):
    columns = jnp.arange(size, dtype=jnp.int32)
    return (target.reshape(-1, 1) == columns[None, :]).astype(BF)


def per_device(amplitudes, integrals, fock_vv, eps_occ, eps_vir, pair_ids, mirror_row):
    pairs, width, vir = amplitudes.shape
    count = lax.axis_size("vir")
    own = amplitudes.transpose(1, 0, 2)
    blocks = lax.axis_size("occ")
    other = lax.ppermute(own, "occ", [(i, i ^ 1) for i in range(blocks)])

    pair = jnp.arange(pairs, dtype=jnp.int32)
    sixteen = jnp.arange(16, dtype=jnp.int32)
    pick = one_hot(sixteen[None, :] * pairs + mirror_row[:, None], 16 * pairs)
    move = one_hot(sixteen[None, :] * pairs + pair[:, None], 16 * pairs)
    part = 15
    steps = jnp.arange(part, dtype=jnp.int32)
    swap = one_hot(steps[:, None] * pairs + mirror_row[None, :], part * pairs)

    occ = jnp.arange(eps_occ.shape[0], dtype=jnp.int32)
    first = jnp.sum(jnp.where(pair_ids[:, 0:1] == occ[None, :], eps_occ[None, :], 0.0), axis=1)
    second = jnp.sum(jnp.where(pair_ids[:, 1:2] == occ[None, :], eps_occ[None, :], 0.0), axis=1)
    local = lax.dynamic_slice_in_dim(eps_vir, lax.axis_index("vir") * width, width)
    rowterm = ((first + second)[None, :] - local[:, None])[:, :, None]
    vir_row = eps_vir[None, :]

    rows_one, rows_two = fprep(fock_vv, count)
    x = xprep(pick, move, own, other)
    got_one = lax.all_to_all(send(rows_one, x, count, width, LO[0]), "vir", 0, 0, tiled=True)
    got_two = lax.all_to_all(send(rows_two, x, count, width, LO[1]), "vir", 0, 0, tiled=True)
    base = right(swap, own, other, integrals.transpose(1, 0, 2), fock_vv, rowterm, vir_row, part)
    base = finish(got_one, rowterm, vir_row, base, LO[0], 0)
    base = finish(got_two, rowterm, vir_row, base, LO[1], LO[0])
    return base.transpose(1, 0, 2)


def solution(mesh):
    return jax.shard_map(
        per_device,
        mesh=mesh,
        in_specs=(
            P("occ", "vir", None),
            P("occ", "vir", None),
            P(),
            P(),
            P(),
            P("occ", None),
            P("occ"),
        ),
        out_specs=P("occ", "vir", None),
        check_vma=False,
    )
```

```python
import functools

import jax
import jax.numpy as jnp
from jax import lax
from jax.experimental import pallas as pl
from jax.experimental.pallas import tpu as pltpu
from jax.sharding import PartitionSpec as P

BF = jnp.bfloat16
F32 = jnp.float32
LANE = 128
HI = 5
LO = (8, 7)
STEP_V = 8
ROWS = STEP_V * HI * 8
HBM = pl.BlockSpec(memory_space=pltpu.HBM)
VMEM = pl.BlockSpec(memory_space=pltpu.VMEM)


def nt(a, b):
    return lax.dot_general(a, b, (((1,), (1,)), ((), ())), preferred_element_type=F32)


def params(mib):
    return pltpu.CompilerParams(vmem_limit_bytes=mib << 20)


def cost(flops, moved):
    return pl.CostEstimate(flops=int(flops), bytes_accessed=int(moved), transcendentals=0)


def resident(x):
    return pltpu.with_memory_space_constraint(x, pltpu.VMEM)


def in_hbm(x):
    return pltpu.with_memory_space_constraint(x, pltpu.HBM)


def pick_rows(width, chunk, g, window, low, high):
    row = lax.broadcasted_iota(jnp.int32, (ROWS, 1), 0)
    dest, hi, lo = row // (HI * 8), (row // 8) % HI, row % 8
    base = sum(LO[:chunk]) * HI
    source = jnp.where(lo < LO[chunk], dest * width + base + lo * HI + hi, -1000)
    col = lax.broadcasted_iota(jnp.int32, (1, high - low), 1) + (low - g * STEP_V * width)
    hot = (source == col).astype(F32).astype(BF)
    return jnp.dot(hot, window, preferred_element_type=F32).astype(BF)


def fprep_kernel(width, chunk, streamed, f_ref, out_ref, *scratch):
    groups = f_ref.shape[0] // width // STEP_V
    span = STEP_V * width
    lows = [g * span // 16 * 16 for g in range(groups)]
    highs = [-(-(g + 1) * span // 16) * 16 for g in range(groups)]
    f_vmem, copies = f_ref, []
    if streamed:
        f_vmem, sems = scratch
        cuts = [0] + highs
        for g in range(groups):
            part = pl.ds(cuts[g], cuts[g + 1] - cuts[g])
            copies.append(pltpu.make_async_copy(f_ref.at[part], f_vmem.at[part], sems.at[g]))
            copies[-1].start()
    for g in range(groups):
        if streamed:
            copies[g].wait()
        window = f_vmem[lows[g] : highs[g], :]
        picked = pick_rows(width, chunk, g, window, lows[g], highs[g])
        out_ref[g * ROWS : (g + 1) * ROWS, :] = picked


def fprep(fock, count, chunk, streamed):
    vir = fock.shape[0]
    groups = count // STEP_V
    scratch = [pltpu.VMEM((vir, vir), BF), pltpu.SemaphoreType.DMA((groups,))]
    return pl.pallas_call(
        functools.partial(fprep_kernel, vir // count, chunk, streamed),
        in_specs=[HBM if streamed else VMEM],
        out_specs=VMEM,
        out_shape=pltpu.VMEM((count * HI * 8, vir), BF),
        scratch_shapes=scratch if streamed else [],
        compiler_params=params(24),
        cost_estimate=cost(4e9, 18e6),
        name="fock_rows",
    )(fock)


def product(width, lo_count, f_ref, x_ref, out_ref, acc0, acc1, stage, wire, sems):
    pairs, pitch, vir = x_ref.shape
    flat = x_ref.reshape(pairs * pitch, vir)
    groups = f_ref.shape[0] // ROWS
    tiles = pairs * pitch // 256
    accs = (acc0, acc1)
    copies = []
    for g in range(groups + 1):
        for n in range(tiles):
            if g < groups:
                accs[g % 2][:, n * 256 : (n + 1) * 256] = nt(
                    f_ref[g * ROWS : (g + 1) * ROWS, :], flat[n * 256 : (n + 1) * 256, :]
                )
            for v in range(n * STEP_V // tiles, (n + 1) * STEP_V // tiles):
                if g > 0:
                    acc = accs[(g + 1) % 2]
                    at = (g - 1) * STEP_V + v
                    pack(width, pairs, pitch, lo_count, acc, v * HI * 8, stage.at[v % 2], wire, at)
        if g > 0:
            part = pl.ds((g - 1) * STEP_V, STEP_V)
            copies.append(pltpu.make_async_copy(wire.at[part], out_ref.at[part], sems.at[g - 1]))
            copies[-1].start()
    for copy in copies:
        copy.wait()


def pack(width, pairs, pitch, lo_count, acc_ref, row, stage_ref, wire_ref, v):
    lane = lax.broadcasted_iota(jnp.int32, (8, LANE), 1)
    tiles = wire_ref.shape[2] // LANE
    for p in range(pairs):
        tile, off = divmod(p * pitch, LANE)
        into = [None] * tiles
        for h in range(HI):
            rows = pl.ds(row + 8 * h, 8)
            seg = acc_ref[rows, tile * LANE : (tile + 1) * LANE]
            if off + width > LANE:
                nxt = acc_ref[rows, (tile + 1) * LANE : (tile + 2) * LANE]
                seg = jnp.where(lane >= off, seg, nxt)
            to, at = divmod(h * width, LANE)
            shift = (at - off) % LANE
            if shift:
                seg = pltpu.roll(seg, shift, 1)
            into[to] = seg if into[to] is None else jnp.where(lane >= at, seg, into[to])
            if at + width > LANE:
                into[to + 1] = seg
        for t in range(tiles):
            stage_ref[t, pl.ds(p, 8, stride=pairs), :] = into[t]
    for t in range(tiles):
        block = stage_ref[t, : lo_count * pairs, :].astype(BF)
        wire_ref[v, :, t * LANE : (t + 1) * LANE] = block


def lead_kernel(
    width, lo_count, pick_ref, move_ref, own, other_ref, f_ref, out_ref, x_ref, x2, sems, other, *scratch
):
    pairs, vir = own.shape[1], own.shape[2]
    starts = range(0, width, 16)
    ins = []
    for j in starts:
        part = pl.ds(j, min(16, width - j))
        ins.append(pltpu.make_async_copy(other_ref.at[part], other.at[part], sems.at[0, j // 16]))
        ins[-1].start()
    outs = []
    for j in starts:
        size = min(16, width - j)
        mine = own[j : j + size].reshape(size * pairs, vir)
        mine = jnp.dot(move_ref[:, : size * pairs], mine, preferred_element_type=F32)
        ins[j // 16].wait()
        theirs = other[j : j + size].reshape(size * pairs, vir)
        theirs = jnp.dot(pick_ref[:, : size * pairs], theirs, preferred_element_type=F32)
        x2[:, j : j + 16, :] = (2.0 * theirs - mine).astype(BF).reshape(pairs, 16, vir)
        part = pl.ds(j, 16)
        outs.append(pltpu.make_async_copy(x2.at[:, part], x_ref.at[:, part], sems.at[1, j // 16]))
        outs[-1].start()
    product(width, lo_count, f_ref, x2, out_ref, *scratch)
    for copy in outs:
        copy.wait()


def send_kernel(width, lo_count, f_ref, x_ref, out_ref, x2, sems, *scratch):
    copy = pltpu.make_async_copy(x_ref, x2, sems.at[0, 0])
    copy.start()
    copy.wait()
    product(width, lo_count, f_ref, x2, out_ref, *scratch)


def wire_call(kernel, name, x_out, args, specs, count, width, pairs, lo_count, vir):
    pitch = -(-width // 16) * 16
    wide = -(-HI * width // LANE) * LANE
    wire = (count, lo_count * pairs, wide)
    out_shape = [pltpu.HBM(wire, BF)]
    out_specs = [HBM]
    blocks = pitch // 16
    scratch = [pltpu.VMEM((pairs, pitch, vir), BF), pltpu.SemaphoreType.DMA((2, blocks))]
    if x_out:
        out_shape.append(pltpu.HBM((pairs, pitch, vir), BF))
        out_specs.append(HBM)
        scratch.append(pltpu.VMEM((width, pairs, vir), BF))
    return pl.pallas_call(
        functools.partial(kernel, width, lo_count),
        in_specs=specs,
        out_specs=out_specs,
        out_shape=out_shape,
        scratch_shapes=scratch
        + [
            pltpu.VMEM((ROWS, pairs * pitch), F32),
            pltpu.VMEM((ROWS, pairs * pitch), F32),
            pltpu.VMEM((2, wide // LANE, 8 * pairs, LANE), F32),
            pltpu.VMEM(wire, BF),
            pltpu.SemaphoreType.DMA((count // STEP_V,)),
        ],
        compiler_params=params(28),
        cost_estimate=cost(2.0 * count * HI * 8 * pairs * pitch * vir, 10e6),
        name=name,
    )(*args)


def right_kernel(skip, count, swap_ref, own_ref, other_ref, int_ref, f_ref, row_ref, vir_ref, *rest):
    out_ref, own, tilde, ints, fock, res, acc0, acc1, f_sems, sems = rest[-10:]
    accs = (acc0, acc1)
    pairs, vir = own.shape[1], own.shape[2]
    rows, step = count * pairs, HI * pairs
    copies = []
    for j in range(count // HI):
        part, here = pl.ds(skip + j * HI, HI), pl.ds(j * HI, HI)
        copies.append(pltpu.make_async_copy(own_ref.at[part], own.at[here], sems.at[0, j]))
        copies.append(pltpu.make_async_copy(other_ref.at[part], tilde.at[here], sems.at[1, j]))
        copies[-2].start()
        copies[-1].start()
    cuts = list(range(0, vir, 256))
    f_copies = []
    for i, n in enumerate(cuts):
        part = pl.ds(n, min(256, vir - n))
        f_copies.append(pltpu.make_async_copy(f_ref.at[part], fock.at[part], f_sems.at[i]))
        f_copies[-1].start()
    int_copy = pltpu.make_async_copy(int_ref.at[pl.ds(skip, count)], ints, sems.at[2, 0])
    int_copy.start()
    for j in range(count // HI):
        copies[2 * j].wait()
        copies[2 * j + 1].wait()
        part = slice(j * HI, (j + 1) * HI)
        theirs = tilde[part].reshape(step, vir)
        theirs = jnp.dot(swap_ref[...], theirs, preferred_element_type=F32)
        mine = own[part].reshape(step, vir).astype(F32)
        tilde[part] = (2.0 * mine - theirs).astype(BF).reshape(HI, pairs, vir)
    int_copy.wait()
    lhs = tilde.reshape(rows, vir)
    for i in range(len(cuts) + 1):
        if i < len(cuts):
            n = cuts[i]
            m = min(n + 256, vir)
            f_copies[i].wait()
            for k in range(0, rows, ROWS):
                part = slice(k, min(k + ROWS, rows))
                accs[i % 2][part, : m - n] = nt(lhs[part, :], fock[n:m, :])
        if i > 0:
            n = cuts[i - 1]
            m = min(n + 256, vir)
            column = vir_ref[:, n:m]
            for k in range(count):
                value = accs[(i + 1) % 2][k * pairs : (k + 1) * pairs, : m - n].astype(BF)
                total = ints[k, :, n:m].astype(F32) + value.astype(F32)
                total = total / (row_ref[skip + k] - column)
                res[k, :, n:m] = own[k, :, n:m].astype(F32) + total
    copy = pltpu.make_async_copy(res, out_ref, sems.at[3, 0])
    copy.start()
    copy.wait()


def right(swap, own, other, integrals, fock, rowterm, vir_row, skip, count, after=None):
    _, pairs, vir = own.shape
    more = [] if after is None else [in_hbm(after)]
    tile = pltpu.VMEM((count, pairs, vir), BF)
    return pl.pallas_call(
        functools.partial(right_kernel, skip, count),
        in_specs=[VMEM] + [HBM] * 4 + [VMEM] * 2 + [HBM] * len(more),
        out_specs=HBM,
        out_shape=pltpu.HBM((count, pairs, vir), F32),
        scratch_shapes=[
            tile,
            tile,
            tile,
            pltpu.VMEM((vir, vir), BF),
            pltpu.VMEM((count, pairs, vir), F32),
            pltpu.VMEM((count * pairs, 256), F32),
            pltpu.VMEM((count * pairs, 256), F32),
            pltpu.SemaphoreType.DMA((-(-vir // 256),)),
            pltpu.SemaphoreType.DMA((4, count // HI)),
        ],
        compiler_params=params(40),
        cost_estimate=cost(2.0 * count * pairs * vir * vir, 20e6),
        name="right_term",
    )(swap, in_hbm(own), in_hbm(other), in_hbm(integrals), in_hbm(fock), rowterm, vir_row, *more)


def finish_kernel(width, skip, got_ref, row_ref, vir_ref, base_ref, *rest):
    out_ref, got, done, sems, got_sems = rest[-5:]
    count = got.shape[0]
    pairs, vir = base_ref.shape[1], base_ref.shape[2]
    lane = lax.broadcasted_iota(jnp.int32, (pairs, LANE), 1)
    tiles = -(-vir // LANE)
    copies, arrive = [], []
    for j in range(base_ref.shape[0] // HI):
        part = pl.ds(j * pairs, pairs)
        arrive.append(pltpu.make_async_copy(got_ref.at[:, part], got.at[:, part], got_sems.at[0, j]))
        arrive[-1].start()
        part = pl.ds(j * HI, HI)
        arrive.append(pltpu.make_async_copy(base_ref.at[part], done.at[part], got_sems.at[1, j]))
        arrive[-1].start()
    for j in range(base_ref.shape[0] // HI):
        rows = slice(j * pairs, (j + 1) * pairs)
        arrive[2 * j].wait()
        arrive[2 * j + 1].wait()
        for h in range(HI):
            src, off = divmod(h * width, LANE)
            a0 = j * HI + h
            into = [None] * (tiles + 1)
            denom = row_ref[skip + a0]

            def put(t):
                a, b = t * LANE, min((t + 1) * LANE, vir)
                value = into[t][:, : b - a] / (denom - vir_ref[:, a:b])
                done[a0, :, a:b] += value

            for w in range(count):
                seg = got[w, rows, src * LANE : (src + 1) * LANE].astype(F32)
                if off + width > LANE:
                    nxt = got[w, rows, (src + 1) * LANE : (src + 2) * LANE].astype(F32)
                    seg = jnp.where(lane >= off, seg, nxt)
                to, at = divmod(w * width, LANE)
                shift = (at - off) % LANE
                if shift:
                    seg = pltpu.roll(seg, shift, 1)
                into[to] = seg if into[to] is None else jnp.where(lane >= at, seg, into[to])
                if at + width > LANE:
                    into[to + 1] = seg
                if at + width >= LANE or w == count - 1:
                    put(to)
                if at + width > LANE and w == count - 1:
                    put(to + 1)
        part = pl.ds(j * HI, HI)
        where = pl.ds(skip + j * HI, HI)
        copies.append(pltpu.make_async_copy(done.at[part], out_ref.at[where], sems.at[j]))
        copies[-1].start()
    for copy in copies:
        copy.wait()


def finish(got, rowterm, vir_row, base, skip, out, width):
    rows, pairs, vir = base.shape
    more = [] if out is None else [in_hbm(out)]
    return pl.pallas_call(
        functools.partial(finish_kernel, width, skip),
        in_specs=[HBM, VMEM, VMEM, HBM] + [HBM] * len(more),
        out_specs=HBM,
        out_shape=pltpu.HBM((width, pairs, vir), F32),
        input_output_aliases={4: 0} if more else {},
        scratch_shapes=[
            pltpu.VMEM(got.shape, BF),
            pltpu.VMEM((rows, pairs, vir), F32),
            pltpu.SemaphoreType.DMA((rows // HI,)),
            pltpu.SemaphoreType.DMA((2, rows // HI)),
        ],
        compiler_params=params(16),
        cost_estimate=cost(1e8, 6e6),
        name="left_add",
    )(got, rowterm, vir_row, in_hbm(base), *more)


def one_hot(target, size):
    columns = jnp.arange(size, dtype=jnp.int32)
    return (target.reshape(-1, 1) == columns[None, :]).astype(BF)


def per_device(amplitudes, integrals, fock_vv, eps_occ, eps_vir, pair_ids, mirror_row):
    pairs, width, vir = amplitudes.shape
    count = lax.axis_size("vir")
    own = amplitudes.transpose(1, 0, 2)
    blocks = lax.axis_size("occ")
    other = lax.ppermute(own, "occ", [(i, i ^ 1) for i in range(blocks)])

    pair = jnp.arange(pairs, dtype=jnp.int32)
    sixteen = jnp.arange(16, dtype=jnp.int32)
    pick = one_hot(sixteen[None, :] * pairs + mirror_row[:, None], 16 * pairs)
    move = one_hot(sixteen[None, :] * pairs + pair[:, None], 16 * pairs)
    swap = one_hot(sixteen[:HI, None] * pairs + mirror_row[None, :], HI * pairs)

    occ = jnp.arange(eps_occ.shape[0], dtype=jnp.int32)
    first = jnp.sum(jnp.where(pair_ids[:, 0:1] == occ[None, :], eps_occ[None, :], 0.0), axis=1)
    second = jnp.sum(jnp.where(pair_ids[:, 1:2] == occ[None, :], eps_occ[None, :], 0.0), axis=1)
    local = lax.dynamic_slice_in_dim(eps_vir, lax.axis_index("vir") * width, width)
    rowterm = ((first + second)[None, :] - local[:, None])[:, :, None]
    vir_row = eps_vir[None, :]

    call = functools.partial(wire_call, count=count, width=width, pairs=pairs, vir=vir)
    rows_one = fprep(in_hbm(fock_vv), count, 0, True)
    args = (pick, move, resident(own), in_hbm(other), rows_one)
    specs = [VMEM, VMEM, VMEM, HBM, VMEM]
    sent_one, x = call(lead_kernel, "left_lead", True, args, specs, lo_count=LO[0])
    got_one = lax.all_to_all(sent_one, "vir", 0, 0, tiled=True)
    rows_two = fprep(in_hbm(fock_vv), count, 1, True)
    args = (rows_two, in_hbm(x))
    (sent_two,) = call(send_kernel, "left_send", False, args, [VMEM, HBM], lo_count=LO[1])
    ints = integrals.transpose(1, 0, 2)
    cut = LO[0] * HI
    args = (swap, own, other, ints, fock_vv, rowterm, vir_row)
    base = right(*args, 0, cut)
    sent_two, base = lax.optimization_barrier((sent_two, base))
    got_two = lax.all_to_all(sent_two, "vir", 0, 0, tiled=True)
    out = finish(got_one, rowterm, vir_row, base, 0, None, width)
    base = right(*args, cut, width - cut, out)
    out = finish(got_two, rowterm, vir_row, base, cut, out, width)
    return out.transpose(1, 0, 2)


def solution(mesh):
    return jax.shard_map(
        per_device,
        mesh=mesh,
        in_specs=(
            P("occ", "vir", None),
            P("occ", "vir", None),
            P(),
            P(),
            P(),
            P("occ", None),
            P("occ"),
        ),
        out_specs=P("occ", "vir", None),
        check_vma=False,
    )
```

```python
import functools

import jax
import jax.numpy as jnp
from jax import lax
from jax.experimental import pallas as pl
from jax.experimental.pallas import tpu as pltpu
from jax.sharding import PartitionSpec as P

BF = jnp.bfloat16
F32 = jnp.float32
LANE = 128
HI = 5
LO = (8, 7)
STEP_V = 8
ROWS = STEP_V * HI * 8
HBM = pl.BlockSpec(memory_space=pltpu.HBM)
VMEM = pl.BlockSpec(memory_space=pltpu.VMEM)
SMEM = pl.BlockSpec(memory_space=pltpu.SMEM)


def nt(a, b):
    return lax.dot_general(a, b, (((1,), (1,)), ((), ())), preferred_element_type=F32)


def params(mib):
    return pltpu.CompilerParams(vmem_limit_bytes=mib << 20)


def cost(flops, moved):
    return pl.CostEstimate(flops=int(flops), bytes_accessed=int(moved), transcendentals=0)


def resident(x):
    return pltpu.with_memory_space_constraint(x, pltpu.VMEM)


def in_hbm(x):
    return pltpu.with_memory_space_constraint(x, pltpu.HBM)


def reorder(pairs, size, mirror_ref=None):
    row = lax.broadcasted_iota(jnp.int32, (16 * pairs, 1), 0)
    pair, at = row // 16, row % 16
    source = pair if mirror_ref is None else mapped(pair, pairs, mirror_ref)
    col = lax.broadcasted_iota(jnp.int32, (1, size * pairs), 1)
    return (at * pairs + source == col).astype(F32).astype(BF)


def mapped(pair, pairs, mirror_ref):
    out = jnp.zeros_like(pair)
    for p in range(pairs):
        out = jnp.where(pair == p, mirror_ref[p], out)
    return out


def pick_rows(width, chunk, g, window, low, high):
    row = lax.broadcasted_iota(jnp.int32, (ROWS, 1), 0)
    dest, hi, lo = row // (HI * 8), (row // 8) % HI, row % 8
    base = sum(LO[:chunk]) * HI
    source = jnp.where(lo < LO[chunk], dest * width + base + lo * HI + hi, -1000)
    col = lax.broadcasted_iota(jnp.int32, (1, high - low), 1) + (low - g * STEP_V * width)
    hot = (source == col).astype(F32).astype(BF)
    return jnp.dot(hot, window, preferred_element_type=F32).astype(BF)


def fprep_kernel(width, chunk, f_ref, *rest):
    moved = chunk == 0
    if moved:
        own_ref, out_ref, mine_ref, f_vmem, sems, own, own_sems = rest
    else:
        out_ref, f_vmem, sems = rest
    groups = f_ref.shape[0] // width // STEP_V
    span = STEP_V * width
    lows = [g * span // 16 * 16 for g in range(groups)]
    highs = [-(-(g + 1) * span // 16) * 16 for g in range(groups)]
    cuts = [0] + highs
    copies, own_copies = [], []
    for g in range(groups):
        part = pl.ds(cuts[g], cuts[g + 1] - cuts[g])
        copies.append(pltpu.make_async_copy(f_ref.at[part], f_vmem.at[part], sems.at[g]))
        copies[-1].start()
    if moved:
        for j in range(0, width, 16):
            part = pl.ds(j, min(16, width - j))
            own_copies.append(pltpu.make_async_copy(own_ref.at[part], own.at[part], own_sems.at[j // 16]))
            own_copies[-1].start()
    for g in range(groups):
        copies[g].wait()
        window = f_vmem[lows[g] : highs[g], :]
        picked = pick_rows(width, chunk, g, window, lows[g], highs[g])
        out_ref[g * ROWS : (g + 1) * ROWS, :] = picked
    if moved:
        pairs, vir = own.shape[1], own.shape[2]
        move = reorder(pairs, 16)
        for j in range(0, width, 16):
            size = min(16, width - j)
            own_copies[j // 16].wait()
            mine = own[j : j + size].reshape(size * pairs, vir)
            mine = jnp.dot(move[:, : size * pairs], mine, preferred_element_type=F32)
            mine_ref[:, j : j + 16, :] = mine.astype(BF).reshape(pairs, 16, vir)


def fprep(fock, count, chunk, own=None):
    vir = fock.shape[0]
    groups = count // STEP_V
    out_shape = [pltpu.VMEM((count * HI * 8, vir), BF)]
    scratch = [pltpu.VMEM((vir, vir), BF), pltpu.SemaphoreType.DMA((groups,))]
    args = [in_hbm(fock)]
    if own is not None:
        width, pairs, _ = own.shape
        blocks = -(-width // 16)
        out_shape.append(pltpu.VMEM((pairs, 16 * blocks, vir), BF))
        scratch += [pltpu.VMEM(own.shape, BF), pltpu.SemaphoreType.DMA((blocks,))]
        args.append(in_hbm(own))
    return pl.pallas_call(
        functools.partial(fprep_kernel, vir // count, chunk),
        in_specs=[HBM] * len(args),
        out_specs=[VMEM] * len(out_shape),
        out_shape=out_shape,
        scratch_shapes=scratch,
        compiler_params=params(30 if own is None else 48),
        cost_estimate=cost(4e9, 18e6),
        name="fock_rows",
    )(*args)


def product(width, lo_count, f_ref, x_ref, out_ref, acc0, acc1, stage, wire, sems):
    pairs, pitch, vir = x_ref.shape
    flat = x_ref.reshape(pairs * pitch, vir)
    groups = f_ref.shape[0] // ROWS
    tiles = pairs * pitch // 256
    accs = (acc0, acc1)
    copies = []
    for g in range(groups + 1):
        for n in range(tiles):
            if g < groups:
                accs[g % 2][:, n * 256 : (n + 1) * 256] = nt(
                    f_ref[g * ROWS : (g + 1) * ROWS, :], flat[n * 256 : (n + 1) * 256, :]
                )
            for v in range(n * STEP_V // tiles, (n + 1) * STEP_V // tiles):
                if g > 0:
                    acc = accs[(g + 1) % 2]
                    at = (g - 1) * STEP_V + v
                    pack(width, pairs, pitch, lo_count, acc, v * HI * 8, stage.at[v % 2], wire, at)
        if g > 0:
            part = pl.ds((g - 1) * STEP_V, STEP_V)
            copies.append(pltpu.make_async_copy(wire.at[part], out_ref.at[part], sems.at[g - 1]))
            copies[-1].start()
    for copy in copies:
        copy.wait()


def pack(width, pairs, pitch, lo_count, acc_ref, row, stage_ref, wire_ref, v):
    lane = lax.broadcasted_iota(jnp.int32, (8, LANE), 1)
    tiles = wire_ref.shape[2] // LANE
    for p in range(pairs):
        tile, off = divmod(p * pitch, LANE)
        into = [None] * tiles
        for h in range(HI):
            rows = pl.ds(row + 8 * h, 8)
            seg = acc_ref[rows, tile * LANE : (tile + 1) * LANE]
            if off + width > LANE:
                nxt = acc_ref[rows, (tile + 1) * LANE : (tile + 2) * LANE]
                seg = jnp.where(lane >= off, seg, nxt)
            to, at = divmod(h * width, LANE)
            shift = (at - off) % LANE
            if shift:
                seg = pltpu.roll(seg, shift, 1)
            into[to] = seg if into[to] is None else jnp.where(lane >= at, seg, into[to])
            if at + width > LANE:
                into[to + 1] = seg
        for t in range(tiles):
            stage_ref[t, pl.ds(p, 8, stride=pairs), :] = into[t]
    for t in range(tiles):
        block = stage_ref[t, : lo_count * pairs, :].astype(BF)
        wire_ref[v, :, t * LANE : (t + 1) * LANE] = block


def lead_kernel(
    width, lo_count, mirror_ref, mine_ref, other_ref, f_ref, out_ref, x_ref, x2, sems, other, *scratch
):
    pairs, vir = other.shape[1], other.shape[2]
    starts = range(0, width, 16)
    ins = []
    for j in starts:
        part = pl.ds(j, min(16, width - j))
        ins.append(pltpu.make_async_copy(other_ref.at[part], other.at[part], sems.at[0, j // 16]))
        ins[-1].start()
    outs = []
    pick = reorder(pairs, 16, mirror_ref)
    for j in starts:
        size = min(16, width - j)
        ins[j // 16].wait()
        theirs = other[j : j + size].reshape(size * pairs, vir)
        theirs = jnp.dot(pick[:, : size * pairs], theirs, preferred_element_type=F32).reshape(pairs, 16, vir)
        mine = mine_ref[:, j : j + 16, :].astype(F32)
        x2[:, j : j + 16, :] = (2.0 * theirs - mine).astype(BF)
        part = pl.ds(j, 16)
        outs.append(pltpu.make_async_copy(x2.at[:, part], x_ref.at[:, part], sems.at[1, j // 16]))
        outs[-1].start()
    product(width, lo_count, f_ref, x2, out_ref, *scratch)
    for copy in outs:
        copy.wait()


def send_kernel(width, lo_count, f_ref, x_ref, out_ref, x2, sems, *scratch):
    copy = pltpu.make_async_copy(x_ref, x2, sems.at[0, 0])
    copy.start()
    copy.wait()
    product(width, lo_count, f_ref, x2, out_ref, *scratch)


def wire_call(kernel, name, x_out, args, specs, count, width, pairs, lo_count, vir):
    pitch = -(-width // 16) * 16
    wide = -(-HI * width // LANE) * LANE
    wire = (count, lo_count * pairs, wide)
    out_shape = [pltpu.HBM(wire, BF)]
    out_specs = [HBM]
    blocks = pitch // 16
    scratch = [pltpu.VMEM((pairs, pitch, vir), BF), pltpu.SemaphoreType.DMA((2, blocks))]
    if x_out:
        out_shape.append(pltpu.HBM((pairs, pitch, vir), BF))
        out_specs.append(HBM)
        scratch.append(pltpu.VMEM((width, pairs, vir), BF))
    return pl.pallas_call(
        functools.partial(kernel, width, lo_count),
        in_specs=specs,
        out_specs=out_specs,
        out_shape=out_shape,
        scratch_shapes=scratch
        + [
            pltpu.VMEM((ROWS, pairs * pitch), F32),
            pltpu.VMEM((ROWS, pairs * pitch), F32),
            pltpu.VMEM((2, wide // LANE, 8 * pairs, LANE), F32),
            pltpu.VMEM(wire, BF),
            pltpu.SemaphoreType.DMA((count // STEP_V,)),
        ],
        compiler_params=params(28),
        cost_estimate=cost(2.0 * count * HI * 8 * pairs * pitch * vir, 10e6),
        name=name,
    )(*args)


def right_kernel(skip, count, mirror_ref, own_ref, other_ref, int_ref, f_ref, row_ref, vir_ref, *rest):
    out_ref, own, tilde, ints, fock, res, acc0, acc1, f_sems, sems = rest[-10:]
    accs = (acc0, acc1)
    pairs, vir = own.shape[1], own.shape[2]
    rows, step = count * pairs, HI * pairs
    copies = []
    for j in range(count // HI):
        part, here = pl.ds(skip + j * HI, HI), pl.ds(j * HI, HI)
        copies.append(pltpu.make_async_copy(own_ref.at[part], own.at[here], sems.at[0, j]))
        copies.append(pltpu.make_async_copy(other_ref.at[part], tilde.at[here], sems.at[1, j]))
        copies[-2].start()
        copies[-1].start()
    int_copy = pltpu.make_async_copy(int_ref.at[pl.ds(skip, count)], ints, sems.at[2, 0])
    int_copy.start()
    cuts = list(range(0, vir, 256))
    f_copies = []
    for i, n in enumerate(cuts):
        part = pl.ds(n, min(256, vir - n))
        f_copies.append(pltpu.make_async_copy(f_ref.at[part], fock.at[part], f_sems.at[i]))
        f_copies[-1].start()
    row = lax.broadcasted_iota(jnp.int32, (step, 1), 0)
    source = row // pairs * pairs + mapped(row % pairs, pairs, mirror_ref)
    swap = (source == lax.broadcasted_iota(jnp.int32, (1, step), 1)).astype(F32).astype(BF)
    for j in range(count // HI):
        copies[2 * j].wait()
        copies[2 * j + 1].wait()
        part = slice(j * HI, (j + 1) * HI)
        theirs = tilde[part].reshape(step, vir)
        theirs = jnp.dot(swap, theirs, preferred_element_type=F32)
        mine = own[part].reshape(step, vir).astype(F32)
        tilde[part] = (2.0 * mine - theirs).astype(BF).reshape(HI, pairs, vir)
    int_copy.wait()
    lhs = tilde.reshape(rows, vir)
    for i in range(len(cuts) + 1):
        if i < len(cuts):
            n = cuts[i]
            m = min(n + 256, vir)
            f_copies[i].wait()
            for k in range(0, rows, ROWS):
                part = slice(k, min(k + ROWS, rows))
                accs[i % 2][part, : m - n] = nt(lhs[part, :], fock[n:m, :])
        if i > 0:
            n = cuts[i - 1]
            m = min(n + 256, vir)
            column = vir_ref[:, n:m]
            for k in range(count):
                value = accs[(i + 1) % 2][k * pairs : (k + 1) * pairs, : m - n].astype(BF)
                total = ints[k, :, n:m].astype(F32) + value.astype(F32)
                total = total / (row_ref[skip + k] - column)
                res[k, :, n:m] = own[k, :, n:m].astype(F32) + total
    copy = pltpu.make_async_copy(res, out_ref, sems.at[3, 0])
    copy.start()
    copy.wait()


def right(mirror, own, other, integrals, fock, rowterm, vir_row, skip, count, after=None):
    _, pairs, vir = own.shape
    more = [] if after is None else [in_hbm(after)]
    tile = pltpu.VMEM((count, pairs, vir), BF)
    return pl.pallas_call(
        functools.partial(right_kernel, skip, count),
        in_specs=[SMEM] + [HBM] * 4 + [VMEM] * 2 + [HBM] * len(more),
        out_specs=HBM,
        out_shape=pltpu.HBM((count, pairs, vir), F32),
        scratch_shapes=[
            tile,
            tile,
            tile,
            pltpu.VMEM((vir, vir), BF),
            pltpu.VMEM((count, pairs, vir), F32),
            pltpu.VMEM((count * pairs, 256), F32),
            pltpu.VMEM((count * pairs, 256), F32),
            pltpu.SemaphoreType.DMA((-(-vir // 256),)),
            pltpu.SemaphoreType.DMA((4, count // HI)),
        ],
        compiler_params=params(40),
        cost_estimate=cost(2.0 * count * pairs * vir * vir, 20e6),
        name="right_term",
    )(mirror, in_hbm(own), in_hbm(other), in_hbm(integrals), in_hbm(fock), rowterm, vir_row, *more)


def finish_kernel(width, skip, got_ref, row_ref, vir_ref, base_ref, *rest):
    out_ref, got, done, sems, got_sems = rest[-5:]
    count = got.shape[0]
    pairs, vir = base_ref.shape[1], base_ref.shape[2]
    lane = lax.broadcasted_iota(jnp.int32, (pairs, LANE), 1)
    tiles = -(-vir // LANE)
    blocks = base_ref.shape[0] // HI

    def arrivals(j):
        rows = pl.ds(pl.multiple_of(j * pairs, 16), pairs)
        part = pl.ds(j * HI, HI)
        return (
            pltpu.make_async_copy(got_ref.at[:, rows], got.at[:, rows], got_sems.at[0, j]),
            pltpu.make_async_copy(base_ref.at[part], done.at[part], got_sems.at[1, j]),
        )

    def leave(j):
        part, where = pl.ds(j * HI, HI), pl.ds(skip + j * HI, HI)
        return pltpu.make_async_copy(done.at[part], out_ref.at[where], sems.at[j])

    for j in range(blocks):
        for copy in arrivals(j):
            copy.start()

    def block(j, carry):
        for copy in arrivals(j):
            copy.wait()
        rows = pl.ds(pl.multiple_of(j * pairs, 16), pairs)
        for h in range(HI):
            src, off = divmod(h * width, LANE)
            a0 = j * HI + h
            into = [None] * (tiles + 1)
            denom = row_ref[skip + a0]

            def put(t):
                a, b = t * LANE, min((t + 1) * LANE, vir)
                value = into[t][:, : b - a] / (denom - vir_ref[:, a:b])
                done[a0, :, a:b] += value

            for w in range(count):
                seg = got[w, rows, src * LANE : (src + 1) * LANE].astype(F32)
                if off + width > LANE:
                    nxt = got[w, rows, (src + 1) * LANE : (src + 2) * LANE].astype(F32)
                    seg = jnp.where(lane >= off, seg, nxt)
                to, at = divmod(w * width, LANE)
                shift = (at - off) % LANE
                if shift:
                    seg = pltpu.roll(seg, shift, 1)
                into[to] = seg if into[to] is None else jnp.where(lane >= at, seg, into[to])
                if at + width > LANE:
                    into[to + 1] = seg
                if at + width >= LANE or w == count - 1:
                    put(to)
                if at + width > LANE and w == count - 1:
                    put(to + 1)
        leave(j).start()
        return carry

    lax.fori_loop(0, blocks, block, 0)
    for j in range(blocks):
        leave(j).wait()


def finish(got, rowterm, vir_row, base, skip, out, width):
    rows, pairs, vir = base.shape
    more = [] if out is None else [in_hbm(out)]
    return pl.pallas_call(
        functools.partial(finish_kernel, width, skip),
        in_specs=[HBM, VMEM, VMEM, HBM] + [HBM] * len(more),
        out_specs=HBM,
        out_shape=pltpu.HBM((width, pairs, vir), F32),
        input_output_aliases={4: 0} if more else {},
        scratch_shapes=[
            pltpu.VMEM(got.shape, BF),
            pltpu.VMEM((rows, pairs, vir), F32),
            pltpu.SemaphoreType.DMA((rows // HI,)),
            pltpu.SemaphoreType.DMA((2, rows // HI)),
        ],
        compiler_params=params(16),
        cost_estimate=cost(1e8, 6e6),
        name="left_add",
    )(got, rowterm, vir_row, in_hbm(base), *more)


def per_device(amplitudes, integrals, fock_vv, eps_occ, eps_vir, pair_ids, mirror_row):
    pairs, width, vir = amplitudes.shape
    count = lax.axis_size("vir")
    own = amplitudes.transpose(1, 0, 2)
    blocks = lax.axis_size("occ")
    other = lax.ppermute(own, "occ", [(i, i ^ 1) for i in range(blocks)])

    call = functools.partial(wire_call, count=count, width=width, pairs=pairs, vir=vir)
    rows_one, mine = fprep(fock_vv, count, 0, own)
    args = (mirror_row, mine, in_hbm(other), rows_one)
    specs = [SMEM, VMEM, HBM, VMEM]
    sent_one, x = call(lead_kernel, "left_lead", True, args, specs, lo_count=LO[0])
    sent_one, eps_occ, eps_vir, pair_ids = lax.optimization_barrier(
        (sent_one, eps_occ, eps_vir, pair_ids)
    )
    got_one = lax.all_to_all(sent_one, "vir", 0, 0, tiled=True)

    occ = jnp.arange(eps_occ.shape[0], dtype=jnp.int32)
    first = jnp.sum(jnp.where(pair_ids[:, 0:1] == occ[None, :], eps_occ[None, :], 0.0), axis=1)
    second = jnp.sum(jnp.where(pair_ids[:, 1:2] == occ[None, :], eps_occ[None, :], 0.0), axis=1)
    local = lax.dynamic_slice_in_dim(eps_vir, lax.axis_index("vir") * width, width)
    rowterm = ((first + second)[None, :] - local[:, None])[:, :, None]
    vir_row = eps_vir[None, :]

    (rows_two,) = fprep(fock_vv, count, 1)
    args = (rows_two, in_hbm(x))
    (sent_two,) = call(send_kernel, "left_send", False, args, [VMEM, HBM], lo_count=LO[1])
    ints = integrals.transpose(1, 0, 2)
    cut = LO[0] * HI
    args = (mirror_row, own, other, ints, fock_vv, rowterm, vir_row)
    base = right(*args, 0, cut)
    sent_two, base = lax.optimization_barrier((sent_two, base))
    got_two = lax.all_to_all(sent_two, "vir", 0, 0, tiled=True)
    out = finish(got_one, rowterm, vir_row, base, 0, None, width)
    base = right(*args, cut, width - cut, out)
    out = finish(got_two, rowterm, vir_row, base, cut, out, width)
    return out.transpose(1, 0, 2)


def solution(mesh):
    return jax.shard_map(
        per_device,
        mesh=mesh,
        in_specs=(
            P("occ", "vir", None),
            P("occ", "vir", None),
            P(),
            P(),
            P(),
            P("occ", None),
            P("occ"),
        ),
        out_specs=P("occ", "vir", None),
        check_vma=False,
    )
```

```python
import functools

import jax
import jax.numpy as jnp
from jax import lax
from jax.experimental import pallas as pl
from jax.experimental.pallas import tpu as pltpu
from jax.sharding import PartitionSpec as P

BF = jnp.bfloat16
F32 = jnp.float32
LANE = 128
HI = 5
LO = (8, 7)
STEP_V = 8
ROWS = STEP_V * HI * 8
HBM = pl.BlockSpec(memory_space=pltpu.HBM)
VMEM = pl.BlockSpec(memory_space=pltpu.VMEM)
SMEM = pl.BlockSpec(memory_space=pltpu.SMEM)


def nt(a, b):
    return lax.dot_general(a, b, (((1,), (1,)), ((), ())), preferred_element_type=F32)


def params(mib):
    return pltpu.CompilerParams(vmem_limit_bytes=mib << 20)


def cost(flops, moved):
    return pl.CostEstimate(flops=int(flops), bytes_accessed=int(moved), transcendentals=0)


def resident(x):
    return pltpu.with_memory_space_constraint(x, pltpu.VMEM)


def in_hbm(x):
    return pltpu.with_memory_space_constraint(x, pltpu.HBM)


def reorder(pairs, size, mirror_ref=None):
    row = lax.broadcasted_iota(jnp.int32, (16 * pairs, 1), 0)
    pair, at = row // 16, row % 16
    source = pair if mirror_ref is None else mapped(pair, pairs, mirror_ref)
    col = lax.broadcasted_iota(jnp.int32, (1, size * pairs), 1)
    return (at * pairs + source == col).astype(F32).astype(BF)


def mapped(pair, pairs, mirror_ref):
    out = jnp.zeros_like(pair)
    for p in range(pairs):
        out = jnp.where(pair == p, mirror_ref[p], out)
    return out


def pick_rows(width, chunk, g, window, low, high):
    row = lax.broadcasted_iota(jnp.int32, (ROWS, 1), 0)
    dest, hi, lo = row // (HI * 8), (row // 8) % HI, row % 8
    base = sum(LO[:chunk]) * HI
    source = jnp.where(lo < LO[chunk], dest * width + base + lo * HI + hi, -1000)
    col = lax.broadcasted_iota(jnp.int32, (1, high - low), 1) + (low - g * STEP_V * width)
    hot = (source == col).astype(F32).astype(BF)
    return jnp.dot(hot, window, preferred_element_type=F32).astype(BF)


def fprep_kernel(width, chunk, f_ref, *rest):
    moved = chunk == 0
    if moved:
        own_ref, out_ref, mine_ref, f_vmem, sems, own, own_sems = rest
    else:
        out_ref, f_vmem, sems = rest
    groups = f_ref.shape[0] // width // STEP_V
    span = STEP_V * width
    lows = [g * span // 16 * 16 for g in range(groups)]
    highs = [-(-(g + 1) * span // 16) * 16 for g in range(groups)]
    cuts = [0] + highs
    copies, own_copies = [], []
    for g in range(groups):
        part = pl.ds(cuts[g], cuts[g + 1] - cuts[g])
        copies.append(pltpu.make_async_copy(f_ref.at[part], f_vmem.at[part], sems.at[g]))
        copies[-1].start()
    if moved:
        for j in range(0, width, 16):
            part = pl.ds(j, min(16, width - j))
            own_copies.append(pltpu.make_async_copy(own_ref.at[part], own.at[part], own_sems.at[j // 16]))
            own_copies[-1].start()
    for g in range(groups):
        copies[g].wait()
        window = f_vmem[lows[g] : highs[g], :]
        picked = pick_rows(width, chunk, g, window, lows[g], highs[g])
        out_ref[g * ROWS : (g + 1) * ROWS, :] = picked
    if moved:
        pairs, vir = own.shape[1], own.shape[2]
        move = reorder(pairs, 16)
        for j in range(0, width, 16):
            size = min(16, width - j)
            own_copies[j // 16].wait()
            mine = own[j : j + size].reshape(size * pairs, vir)
            mine = jnp.dot(move[:, : size * pairs], mine, preferred_element_type=F32)
            mine_ref[:, j : j + 16, :] = mine.astype(BF).reshape(pairs, 16, vir)


def fprep(fock, count, chunk, own=None):
    vir = fock.shape[0]
    groups = count // STEP_V
    out_shape = [pltpu.VMEM((count * HI * 8, vir), BF)]
    scratch = [pltpu.VMEM((vir, vir), BF), pltpu.SemaphoreType.DMA((groups,))]
    args = [in_hbm(fock)]
    if own is not None:
        width, pairs, _ = own.shape
        blocks = -(-width // 16)
        out_shape.append(pltpu.VMEM((pairs, 16 * blocks, vir), BF))
        scratch += [pltpu.VMEM(own.shape, BF), pltpu.SemaphoreType.DMA((blocks,))]
        args.append(in_hbm(own))
    return pl.pallas_call(
        functools.partial(fprep_kernel, vir // count, chunk),
        in_specs=[HBM] * len(args),
        out_specs=[VMEM] * len(out_shape),
        out_shape=out_shape,
        scratch_shapes=scratch,
        compiler_params=params(30 if own is None else 48),
        cost_estimate=cost(4e9, 18e6),
        name="fock_rows",
    )(*args)


def product_straight(width, lo_count, f_ref, x_ref, out_ref, acc0, acc1, stage, wire, sems):
    pairs, pitch, vir = x_ref.shape
    flat = x_ref.reshape(pairs * pitch, vir)
    groups = f_ref.shape[0] // ROWS
    tiles = pairs * pitch // 256
    accs = (acc0, acc1)
    copies = []
    for g in range(groups + 1):
        for n in range(tiles):
            if g < groups:
                accs[g % 2][:, n * 256 : (n + 1) * 256] = nt(
                    f_ref[g * ROWS : (g + 1) * ROWS, :], flat[n * 256 : (n + 1) * 256, :]
                )
            for v in range(n * STEP_V // tiles, (n + 1) * STEP_V // tiles):
                if g > 0:
                    acc = accs[(g + 1) % 2]
                    at = (g - 1) * STEP_V + v
                    pack(width, pairs, pitch, lo_count, acc, v * HI * 8, stage.at[v % 2], wire, at)
        if g > 0:
            part = pl.ds((g - 1) * STEP_V, STEP_V)
            copies.append(pltpu.make_async_copy(wire.at[part], out_ref.at[part], sems.at[g - 1]))
            copies[-1].start()
    for copy in copies:
        copy.wait()


def product(width, lo_count, f_ref, x_ref, out_ref, acc0, acc1, stage, wire, sems):
    pairs, pitch, vir = x_ref.shape
    flat = x_ref.reshape(pairs * pitch, vir)
    groups = f_ref.shape[0] // ROWS
    tiles = pairs * pitch // 256
    accs = (acc0, acc1)

    def multiply(g, n):
        lanes = pl.ds(pl.multiple_of(n * 256, 256), 256)
        accs[g % 2][:, lanes] = nt(f_ref[g * ROWS : (g + 1) * ROWS, :], flat[lanes, :])

    def packed(g, v, slot):
        row = pl.multiple_of(v * (HI * 8), 8)
        pack(width, pairs, pitch, lo_count, accs[g % 2], row, stage.at[slot], wire, g * STEP_V + v)

    def leave(g):
        part = pl.ds(g * STEP_V, STEP_V)
        return pltpu.make_async_copy(wire.at[part], out_ref.at[part], sems.at[g])

    for g in range(groups):

        def step(n, carry, g=g):
            multiply(g, n)
            if g > 0:
                packed(g - 1, n, 0)
                packed(g - 1, jnp.minimum(tiles + n, STEP_V - 1), 1)
            return carry

        lax.fori_loop(0, tiles, step, 0)
        if g > 0:
            leave(g - 1).start()

    def last(n, carry):
        packed(groups - 1, 2 * n, 0)
        packed(groups - 1, 2 * n + 1, 1)
        return carry

    lax.fori_loop(0, STEP_V // 2, last, 0)
    leave(groups - 1).start()
    for g in range(groups):
        leave(g).wait()


def pack(width, pairs, pitch, lo_count, acc_ref, row, stage_ref, wire_ref, v):
    lane = lax.broadcasted_iota(jnp.int32, (8, LANE), 1)
    tiles = wire_ref.shape[2] // LANE
    for p in range(pairs):
        tile, off = divmod(p * pitch, LANE)
        into = [None] * tiles
        for h in range(HI):
            rows = pl.ds(pl.multiple_of(row + 8 * h, 8), 8)
            seg = acc_ref[rows, tile * LANE : (tile + 1) * LANE]
            if off + width > LANE:
                nxt = acc_ref[rows, (tile + 1) * LANE : (tile + 2) * LANE]
                seg = jnp.where(lane >= off, seg, nxt)
            to, at = divmod(h * width, LANE)
            shift = (at - off) % LANE
            if shift:
                seg = pltpu.roll(seg, shift, 1)
            into[to] = seg if into[to] is None else jnp.where(lane >= at, seg, into[to])
            if at + width > LANE:
                into[to + 1] = seg
        for t in range(tiles):
            stage_ref[t, pl.ds(p, 8, stride=pairs), :] = into[t]
    for t in range(tiles):
        block = stage_ref[t, : lo_count * pairs, :].astype(BF)
        wire_ref[v, :, t * LANE : (t + 1) * LANE] = block


def lead_kernel(
    width, lo_count, mirror_ref, mine_ref, other_ref, f_ref, out_ref, x_ref, x2, sems, other, *scratch
):
    pairs, vir = other.shape[1], other.shape[2]
    starts = range(0, width, 16)
    ins = []
    for j in starts:
        part = pl.ds(j, min(16, width - j))
        ins.append(pltpu.make_async_copy(other_ref.at[part], other.at[part], sems.at[0, j // 16]))
        ins[-1].start()
    outs = []
    pick = reorder(pairs, 16, mirror_ref)
    for j in starts:
        size = min(16, width - j)
        ins[j // 16].wait()
        theirs = other[j : j + size].reshape(size * pairs, vir)
        theirs = jnp.dot(pick[:, : size * pairs], theirs, preferred_element_type=F32).reshape(pairs, 16, vir)
        mine = mine_ref[:, j : j + 16, :].astype(F32)
        x2[:, j : j + 16, :] = (2.0 * theirs - mine).astype(BF)
        part = pl.ds(j, 16)
        outs.append(pltpu.make_async_copy(x2.at[:, part], x_ref.at[:, part], sems.at[1, j // 16]))
        outs[-1].start()
    product_straight(width, lo_count, f_ref, x2, out_ref, *scratch)
    for copy in outs:
        copy.wait()


def send_kernel(width, lo_count, f_ref, x_ref, out_ref, x2, sems, *scratch):
    copy = pltpu.make_async_copy(x_ref, x2, sems.at[0, 0])
    copy.start()
    copy.wait()
    product(width, lo_count, f_ref, x2, out_ref, *scratch)


def wire_call(kernel, name, x_out, args, specs, count, width, pairs, lo_count, vir):
    pitch = -(-width // 16) * 16
    wide = -(-HI * width // LANE) * LANE
    wire = (count, lo_count * pairs, wide)
    out_shape = [pltpu.HBM(wire, BF)]
    out_specs = [HBM]
    blocks = pitch // 16
    scratch = [pltpu.VMEM((pairs, pitch, vir), BF), pltpu.SemaphoreType.DMA((2, blocks))]
    if x_out:
        out_shape.append(pltpu.HBM((pairs, pitch, vir), BF))
        out_specs.append(HBM)
        scratch.append(pltpu.VMEM((width, pairs, vir), BF))
    return pl.pallas_call(
        functools.partial(kernel, width, lo_count),
        in_specs=specs,
        out_specs=out_specs,
        out_shape=out_shape,
        scratch_shapes=scratch
        + [
            pltpu.VMEM((ROWS, pairs * pitch), F32),
            pltpu.VMEM((ROWS, pairs * pitch), F32),
            pltpu.VMEM((2, wide // LANE, 8 * pairs, LANE), F32),
            pltpu.VMEM(wire, BF),
            pltpu.SemaphoreType.DMA((count // STEP_V,)),
        ],
        compiler_params=params(28),
        cost_estimate=cost(2.0 * count * HI * 8 * pairs * pitch * vir, 10e6),
        name=name,
    )(*args)


def right_kernel(swap_ref, own_ref, other_ref, int_ref, f_ref, row_ref, vir_ref, out_ref):
    part, pairs, vir = own_ref.shape
    rows = part * pairs
    own = own_ref[...].reshape(rows, vir)
    other = other_ref[...].reshape(rows, vir)
    theirs = jnp.dot(swap_ref[...], other, preferred_element_type=F32)
    tilde = (2.0 * own.astype(F32) - theirs).astype(BF)
    for n in range(0, vir, 512):
        m = min(n + 512, vir)
        right = nt(tilde, f_ref[n:m, :]).astype(BF).astype(F32)
        denom = row_ref[...].reshape(rows, 1) - vir_ref[:, n:m]
        total = int_ref[:, :, n:m].reshape(rows, m - n).astype(F32) + right
        res = own_ref[:, :, n:m].reshape(rows, m - n).astype(F32) + total / denom
        out_ref[:, :, n:m] = res.reshape(part, pairs, m - n)


def right(swap, own, other, integrals, fock, rowterm, vir_row, part=15):
    width, pairs, vir = own.shape
    block = pl.BlockSpec((part, pairs, vir), lambda j: (j, 0, 0))
    return pl.pallas_call(
        right_kernel,
        grid=(width // part,),
        in_specs=[
            pl.BlockSpec((part * pairs, part * pairs), lambda j: (0, 0)),
            block,
            block,
            block,
            pl.BlockSpec((vir, vir), lambda j: (0, 0)),
            pl.BlockSpec((part, pairs, 1), lambda j: (j, 0, 0)),
            pl.BlockSpec((1, vir), lambda j: (0, 0)),
        ],
        out_specs=block,
        out_shape=jax.ShapeDtypeStruct((width, pairs, vir), F32),
        compiler_params=params(56),
        cost_estimate=cost(2.0 * width * pairs * vir * vir, 40e6),
        name="right_term",
    )(swap, own, other, integrals, fock, rowterm, vir_row)


def finish_kernel(
    width, skip, got_ref, row_ref, vir_ref, base_ref, out_ref, got, done, sems, got_sems
):
    count = got.shape[0]
    pairs, vir = base_ref.shape[1], base_ref.shape[2]
    lane = lax.broadcasted_iota(jnp.int32, (pairs, LANE), 1)
    tiles = -(-vir // LANE)
    blocks = done.shape[0] // HI

    def arrivals(j):
        rows = pl.ds(pl.multiple_of(j * pairs, 16), pairs)
        part, where = pl.ds(j * HI, HI), pl.ds(skip + j * HI, HI)
        return (
            pltpu.make_async_copy(got_ref.at[:, rows], got.at[:, rows], got_sems.at[0, j]),
            pltpu.make_async_copy(base_ref.at[where], done.at[part], got_sems.at[1, j]),
        )

    def leave(j):
        part, where = pl.ds(j * HI, HI), pl.ds(skip + j * HI, HI)
        return pltpu.make_async_copy(done.at[part], out_ref.at[where], sems.at[j])

    for j in range(blocks):
        for copy in arrivals(j):
            copy.start()

    def block(j, carry):
        for copy in arrivals(j):
            copy.wait()
        rows = pl.ds(pl.multiple_of(j * pairs, 16), pairs)
        for h in range(HI):
            src, off = divmod(h * width, LANE)
            a0 = j * HI + h
            into = [None] * (tiles + 1)
            denom = row_ref[skip + a0]

            def put(t):
                a, b = t * LANE, min((t + 1) * LANE, vir)
                value = into[t][:, : b - a] / (denom - vir_ref[:, a:b])
                done[a0, :, a:b] += value

            for w in range(count):
                seg = got[w, rows, src * LANE : (src + 1) * LANE].astype(F32)
                if off + width > LANE:
                    nxt = got[w, rows, (src + 1) * LANE : (src + 2) * LANE].astype(F32)
                    seg = jnp.where(lane >= off, seg, nxt)
                to, at = divmod(w * width, LANE)
                shift = (at - off) % LANE
                if shift:
                    seg = pltpu.roll(seg, shift, 1)
                into[to] = seg if into[to] is None else jnp.where(lane >= at, seg, into[to])
                if at + width > LANE:
                    into[to + 1] = seg
                if at + width >= LANE or w == count - 1:
                    put(to)
                if at + width > LANE and w == count - 1:
                    put(to + 1)
        leave(j).start()
        return carry

    lax.fori_loop(0, blocks, block, 0)
    for j in range(blocks):
        leave(j).wait()


def finish(got, rowterm, vir_row, base, skip, rows):
    width, pairs, vir = base.shape
    return pl.pallas_call(
        functools.partial(finish_kernel, width, skip),
        in_specs=[HBM, VMEM, VMEM, HBM],
        out_specs=HBM,
        out_shape=pltpu.HBM((width, pairs, vir), F32),
        input_output_aliases={3: 0},
        scratch_shapes=[
            pltpu.VMEM(got.shape, BF),
            pltpu.VMEM((rows, pairs, vir), F32),
            pltpu.SemaphoreType.DMA((rows // HI,)),
            pltpu.SemaphoreType.DMA((2, rows // HI)),
        ],
        compiler_params=params(16),
        cost_estimate=cost(1e8, 16e6),
        name="left_add",
    )(got, rowterm, vir_row, in_hbm(base))


def per_device(amplitudes, integrals, fock_vv, eps_occ, eps_vir, pair_ids, mirror_row):
    pairs, width, vir = amplitudes.shape
    count = lax.axis_size("vir")
    own = amplitudes.transpose(1, 0, 2)
    blocks = lax.axis_size("occ")
    other = lax.ppermute(own, "occ", [(i, i ^ 1) for i in range(blocks)])

    call = functools.partial(wire_call, count=count, width=width, pairs=pairs, vir=vir)
    rows_one, mine = fprep(fock_vv, count, 0, own)
    args = (mirror_row, mine, in_hbm(other), rows_one)
    specs = [SMEM, VMEM, HBM, VMEM]
    sent_one, x = call(lead_kernel, "left_lead", True, args, specs, lo_count=LO[0])
    sent_one, eps_occ, eps_vir, pair_ids, mirror = lax.optimization_barrier(
        (sent_one, eps_occ, eps_vir, pair_ids, mirror_row)
    )
    got_one = lax.all_to_all(sent_one, "vir", 0, 0, tiled=True)

    occ = jnp.arange(eps_occ.shape[0], dtype=jnp.int32)
    first = jnp.sum(jnp.where(pair_ids[:, 0:1] == occ[None, :], eps_occ[None, :], 0.0), axis=1)
    second = jnp.sum(jnp.where(pair_ids[:, 1:2] == occ[None, :], eps_occ[None, :], 0.0), axis=1)
    local = lax.dynamic_slice_in_dim(eps_vir, lax.axis_index("vir") * width, width)
    rowterm = ((first + second)[None, :] - local[:, None])[:, :, None]
    vir_row = eps_vir[None, :]

    (rows_two,) = fprep(fock_vv, count, 1)
    args = (rows_two, in_hbm(x))
    (sent_two,) = call(send_kernel, "left_send", False, args, [VMEM, HBM], lo_count=LO[1])
    got_two = lax.all_to_all(sent_two, "vir", 0, 0, tiled=True)
    ints = integrals.transpose(1, 0, 2)
    part, cut = 15, LO[0] * HI
    source = jnp.arange(part, dtype=jnp.int32)[:, None] * pairs + mirror[None, :]
    swap = (source.reshape(-1, 1) == jnp.arange(part * pairs, dtype=jnp.int32)).astype(BF)
    base = right(swap, own, other, ints, fock_vv, rowterm, vir_row, part)
    out = finish(got_one, rowterm, vir_row, base, 0, cut)
    out = finish(got_two, rowterm, vir_row, out, cut, width - cut)
    return out.transpose(1, 0, 2)


def solution(mesh):
    return jax.shard_map(
        per_device,
        mesh=mesh,
        in_specs=(
            P("occ", "vir", None),
            P("occ", "vir", None),
            P(),
            P(),
            P(),
            P("occ", None),
            P("occ"),
        ),
        out_specs=P("occ", "vir", None),
        check_vma=False,
    )
```

```python
import functools

import jax
import jax.numpy as jnp
from jax import lax
from jax.experimental import pallas as pl
from jax.experimental.pallas import tpu as pltpu
from jax.sharding import PartitionSpec as P

BF = jnp.bfloat16
F32 = jnp.float32
LANE = 128
HI = 5
LO = (8, 7)
STEP_V = 8
ROWS = STEP_V * HI * 8
HBM = pl.BlockSpec(memory_space=pltpu.HBM)
VMEM = pl.BlockSpec(memory_space=pltpu.VMEM)
SMEM = pl.BlockSpec(memory_space=pltpu.SMEM)


def nt(a, b):
    return lax.dot_general(a, b, (((1,), (1,)), ((), ())), preferred_element_type=F32)


def params(mib):
    return pltpu.CompilerParams(vmem_limit_bytes=mib << 20)


def cost(flops, moved):
    return pl.CostEstimate(flops=int(flops), bytes_accessed=int(moved), transcendentals=0)


def resident(x):
    return pltpu.with_memory_space_constraint(x, pltpu.VMEM)


def in_hbm(x):
    return pltpu.with_memory_space_constraint(x, pltpu.HBM)


def reorder(pairs, size, mirror_ref=None):
    row = lax.broadcasted_iota(jnp.int32, (16 * pairs, 1), 0)
    pair, at = row // 16, row % 16
    source = pair if mirror_ref is None else mapped(pair, pairs, mirror_ref)
    col = lax.broadcasted_iota(jnp.int32, (1, size * pairs), 1)
    return (at * pairs + source == col).astype(F32).astype(BF)


def mapped(pair, pairs, mirror_ref):
    out = jnp.zeros_like(pair)
    for p in range(pairs):
        out = jnp.where(pair == p, mirror_ref[p], out)
    return out


def pick_rows(width, chunk, g, window, low, high):
    row = lax.broadcasted_iota(jnp.int32, (ROWS, 1), 0)
    dest, hi, lo = row // (HI * 8), (row // 8) % HI, row % 8
    base = sum(LO[:chunk]) * HI
    source = jnp.where(lo < LO[chunk], dest * width + base + lo * HI + hi, -1000)
    col = lax.broadcasted_iota(jnp.int32, (1, high - low), 1) + (low - g * STEP_V * width)
    hot = (source == col).astype(F32).astype(BF)
    return jnp.dot(hot, window, preferred_element_type=F32).astype(BF)


def fprep_kernel(width, chunk, f_ref, *rest):
    moved = chunk == 0
    if moved:
        own_ref, out_ref, mine_ref, f_vmem, sems, own, own_sems = rest
    else:
        out_ref, f_vmem, sems = rest
    groups = f_ref.shape[0] // width // STEP_V
    span = STEP_V * width
    lows = [g * span // 16 * 16 for g in range(groups)]
    highs = [-(-(g + 1) * span // 16) * 16 for g in range(groups)]
    cuts = [0] + highs
    copies, own_copies = [], []
    if moved:
        for j in range(0, width, 16):
            part = pl.ds(j, min(16, width - j))
            own_copies.append(pltpu.make_async_copy(own_ref.at[part], own.at[part], own_sems.at[j // 16]))
            own_copies[-1].start()
    for g in range(groups):
        part = pl.ds(cuts[g], cuts[g + 1] - cuts[g])
        copies.append(pltpu.make_async_copy(f_ref.at[part], f_vmem.at[part], sems.at[g]))
        copies[-1].start()
    if moved:
        pairs, vir = own.shape[1], own.shape[2]
        move = reorder(pairs, 16)
        for j in range(0, width, 16):
            size = min(16, width - j)
            own_copies[j // 16].wait()
            mine = own[j : j + size].reshape(size * pairs, vir)
            mine = jnp.dot(move[:, : size * pairs], mine, preferred_element_type=F32)
            mine_ref[:, j : j + 16, :] = mine.astype(BF).reshape(pairs, 16, vir)
    for g in range(groups):
        copies[g].wait()
        window = f_vmem[lows[g] : highs[g], :]
        picked = pick_rows(width, chunk, g, window, lows[g], highs[g])
        out_ref[g * ROWS : (g + 1) * ROWS, :] = picked


def fprep(fock, count, chunk, own=None):
    vir = fock.shape[0]
    groups = count // STEP_V
    out_shape = [pltpu.VMEM((count * HI * 8, vir), BF)]
    scratch = [pltpu.VMEM((vir, vir), BF), pltpu.SemaphoreType.DMA((groups,))]
    args = [in_hbm(fock)]
    if own is not None:
        width, pairs, _ = own.shape
        blocks = -(-width // 16)
        out_shape.append(pltpu.VMEM((pairs, 16 * blocks, vir), BF))
        scratch += [pltpu.VMEM(own.shape, BF), pltpu.SemaphoreType.DMA((blocks,))]
        args.append(in_hbm(own))
    return pl.pallas_call(
        functools.partial(fprep_kernel, vir // count, chunk),
        in_specs=[HBM] * len(args),
        out_specs=[VMEM] * len(out_shape),
        out_shape=out_shape,
        scratch_shapes=scratch,
        compiler_params=params(30 if own is None else 48),
        cost_estimate=cost(4e9, 18e6),
        name="fock_rows",
    )(*args)


def product_straight(width, lo_count, f_ref, x_ref, out_ref, acc0, acc1, stage, wire, sems):
    pairs, pitch, vir = x_ref.shape
    flat = x_ref.reshape(pairs * pitch, vir)
    groups = f_ref.shape[0] // ROWS
    tiles = pairs * pitch // 256
    accs = (acc0, acc1)
    copies = []
    for g in range(groups + 1):
        for n in range(tiles):
            if g < groups:
                accs[g % 2][:, n * 256 : (n + 1) * 256] = nt(
                    f_ref[g * ROWS : (g + 1) * ROWS, :], flat[n * 256 : (n + 1) * 256, :]
                )
            for v in range(n * STEP_V // tiles, (n + 1) * STEP_V // tiles):
                if g > 0:
                    acc = accs[(g + 1) % 2]
                    at = (g - 1) * STEP_V + v
                    pack(width, pairs, pitch, lo_count, acc, v * HI * 8, stage.at[v % 2], wire, at)
        if g > 0:
            part = pl.ds((g - 1) * STEP_V, STEP_V)
            copies.append(pltpu.make_async_copy(wire.at[part], out_ref.at[part], sems.at[g - 1]))
            copies[-1].start()
    for copy in copies:
        copy.wait()


def product(width, lo_count, f_ref, x_ref, out_ref, acc0, acc1, stage, wire, sems):
    pairs, pitch, vir = x_ref.shape
    flat = x_ref.reshape(pairs * pitch, vir)
    groups = f_ref.shape[0] // ROWS
    tiles = pairs * pitch // 256
    accs = (acc0, acc1)

    def multiply(g, n):
        lanes = pl.ds(pl.multiple_of(n * 256, 256), 256)
        accs[g % 2][:, lanes] = nt(f_ref[g * ROWS : (g + 1) * ROWS, :], flat[lanes, :])

    def packed(g, v, slot):
        row = pl.multiple_of(v * (HI * 8), 8)
        pack(width, pairs, pitch, lo_count, accs[g % 2], row, stage.at[slot], wire, g * STEP_V + v)

    def leave(g):
        part = pl.ds(g * STEP_V, STEP_V)
        return pltpu.make_async_copy(wire.at[part], out_ref.at[part], sems.at[g])

    for g in range(groups):

        def step(n, carry, g=g):
            multiply(g, n)
            if g > 0:
                packed(g - 1, n, 0)
                packed(g - 1, jnp.minimum(tiles + n, STEP_V - 1), 1)
            return carry

        lax.fori_loop(0, tiles, step, 0)
        if g > 0:
            leave(g - 1).start()

    def last(n, carry):
        packed(groups - 1, 2 * n, 0)
        packed(groups - 1, 2 * n + 1, 1)
        return carry

    lax.fori_loop(0, STEP_V // 2, last, 0)
    leave(groups - 1).start()
    for g in range(groups):
        leave(g).wait()


def pack(width, pairs, pitch, lo_count, acc_ref, row, stage_ref, wire_ref, v):
    lane = lax.broadcasted_iota(jnp.int32, (8, LANE), 1)
    tiles = wire_ref.shape[2] // LANE
    for p in range(pairs):
        tile, off = divmod(p * pitch, LANE)
        into = [None] * tiles
        for h in range(HI):
            rows = pl.ds(pl.multiple_of(row + 8 * h, 8), 8)
            seg = acc_ref[rows, tile * LANE : (tile + 1) * LANE]
            if off + width > LANE:
                nxt = acc_ref[rows, (tile + 1) * LANE : (tile + 2) * LANE]
                seg = jnp.where(lane >= off, seg, nxt)
            to, at = divmod(h * width, LANE)
            shift = (at - off) % LANE
            if shift:
                seg = pltpu.roll(seg, shift, 1)
            into[to] = seg if into[to] is None else jnp.where(lane >= at, seg, into[to])
            if at + width > LANE:
                into[to + 1] = seg
        for t in range(tiles):
            stage_ref[t, pl.ds(p, 8, stride=pairs), :] = into[t]
    for t in range(tiles):
        block = stage_ref[t, : lo_count * pairs, :].astype(BF)
        wire_ref[v, :, t * LANE : (t + 1) * LANE] = block


def lead_kernel(
    width, lo_count, mirror_ref, mine_ref, other_ref, f_ref, out_ref, x_ref, x2, sems, other, *scratch
):
    pairs, vir = other.shape[1], other.shape[2]
    starts = range(0, width, 16)
    ins = []
    for j in starts:
        part = pl.ds(j, min(16, width - j))
        ins.append(pltpu.make_async_copy(other_ref.at[part], other.at[part], sems.at[0, j // 16]))
        ins[-1].start()
    outs = []
    pick = reorder(pairs, 16, mirror_ref)
    for j in starts:
        size = min(16, width - j)
        ins[j // 16].wait()
        theirs = other[j : j + size].reshape(size * pairs, vir)
        theirs = jnp.dot(pick[:, : size * pairs], theirs, preferred_element_type=F32).reshape(pairs, 16, vir)
        mine = mine_ref[:, j : j + 16, :].astype(F32)
        x2[:, j : j + 16, :] = (2.0 * theirs - mine).astype(BF)
        part = pl.ds(j, 16)
        outs.append(pltpu.make_async_copy(x2.at[:, part], x_ref.at[:, part], sems.at[1, j // 16]))
        outs[-1].start()
    product_straight(width, lo_count, f_ref, x2, out_ref, *scratch)
    for copy in outs:
        copy.wait()


def send_kernel(width, lo_count, f_ref, x_ref, out_ref, x2, sems, *scratch):
    copy = pltpu.make_async_copy(x_ref, x2, sems.at[0, 0])
    copy.start()
    copy.wait()
    product(width, lo_count, f_ref, x2, out_ref, *scratch)


def wire_call(kernel, name, x_out, args, specs, count, width, pairs, lo_count, vir):
    pitch = -(-width // 16) * 16
    wide = -(-HI * width // LANE) * LANE
    wire = (count, lo_count * pairs, wide)
    out_shape = [pltpu.HBM(wire, BF)]
    out_specs = [HBM]
    blocks = pitch // 16
    scratch = [pltpu.VMEM((pairs, pitch, vir), BF), pltpu.SemaphoreType.DMA((2, blocks))]
    if x_out:
        out_shape.append(pltpu.HBM((pairs, pitch, vir), BF))
        out_specs.append(HBM)
        scratch.append(pltpu.VMEM((width, pairs, vir), BF))
    return pl.pallas_call(
        functools.partial(kernel, width, lo_count),
        in_specs=specs,
        out_specs=out_specs,
        out_shape=out_shape,
        scratch_shapes=scratch
        + [
            pltpu.VMEM((ROWS, pairs * pitch), F32),
            pltpu.VMEM((ROWS, pairs * pitch), F32),
            pltpu.VMEM((2, wide // LANE, 8 * pairs, LANE), F32),
            pltpu.VMEM(wire, BF),
            pltpu.SemaphoreType.DMA((count // STEP_V,)),
        ],
        compiler_params=params(28),
        cost_estimate=cost(2.0 * count * HI * 8 * pairs * pitch * vir, 10e6),
        name=name,
    )(*args)


def right_kernel(swap_ref, own_ref, other_ref, int_ref, f_ref, row_ref, vir_ref, out_ref):
    part, pairs, vir = own_ref.shape
    rows = part * pairs
    own = own_ref[...].reshape(rows, vir)
    other = other_ref[...].reshape(rows, vir)
    theirs = jnp.dot(swap_ref[...], other, preferred_element_type=F32)
    tilde = (2.0 * own.astype(F32) - theirs).astype(BF)
    for n in range(0, vir, 512):
        m = min(n + 512, vir)
        right = nt(tilde, f_ref[n:m, :]).astype(BF).astype(F32)
        denom = row_ref[...].reshape(rows, 1) - vir_ref[:, n:m]
        total = int_ref[:, :, n:m].reshape(rows, m - n).astype(F32) + right
        res = own_ref[:, :, n:m].reshape(rows, m - n).astype(F32) + total / denom
        out_ref[:, :, n:m] = res.reshape(part, pairs, m - n)


def right(swap, own, other, integrals, fock, rowterm, vir_row, part=15):
    width, pairs, vir = own.shape
    block = pl.BlockSpec((part, pairs, vir), lambda j: (j, 0, 0))
    return pl.pallas_call(
        right_kernel,
        grid=(width // part,),
        in_specs=[
            pl.BlockSpec((part * pairs, part * pairs), lambda j: (0, 0)),
            block,
            block,
            block,
            pl.BlockSpec((vir, vir), lambda j: (0, 0), pipeline_mode=pl.Buffered(1)),
            pl.BlockSpec((part, pairs, 1), lambda j: (j, 0, 0)),
            pl.BlockSpec((1, vir), lambda j: (0, 0)),
        ],
        out_specs=block,
        out_shape=jax.ShapeDtypeStruct((width, pairs, vir), F32),
        compiler_params=params(36),
        cost_estimate=cost(2.0 * width * pairs * vir * vir, 40e6),
        name="right_term",
    )(swap, in_hbm(own), in_hbm(other), in_hbm(integrals), in_hbm(fock), rowterm, vir_row)


def finish_kernel(
    width, skip, got_ref, row_hbm, vir_ref, base_ref, out_ref, got, done, row_ref, sems, got_sems, row_sem
):
    row_copy = pltpu.make_async_copy(row_hbm.at[pl.ds(skip, done.shape[0])], row_ref, row_sem)
    row_copy.start()
    count = got.shape[0]
    pairs, vir = base_ref.shape[1], base_ref.shape[2]
    lane = lax.broadcasted_iota(jnp.int32, (pairs, LANE), 1)
    tiles = -(-vir // LANE)
    blocks = done.shape[0] // HI

    def arrivals(j):
        rows = pl.ds(pl.multiple_of(j * pairs, 16), pairs)
        part, where = pl.ds(j * HI, HI), pl.ds(skip + j * HI, HI)
        return (
            pltpu.make_async_copy(got_ref.at[:, rows], got.at[:, rows], got_sems.at[0, j]),
            pltpu.make_async_copy(base_ref.at[where], done.at[part], got_sems.at[1, j]),
        )

    def leave(j):
        part, where = pl.ds(j * HI, HI), pl.ds(skip + j * HI, HI)
        return pltpu.make_async_copy(done.at[part], out_ref.at[where], sems.at[j])

    for j in range(blocks):
        for copy in arrivals(j):
            copy.start()
    row_copy.wait()

    def block(j, carry):
        for copy in arrivals(j):
            copy.wait()
        rows = pl.ds(pl.multiple_of(j * pairs, 16), pairs)
        for h in range(HI):
            src, off = divmod(h * width, LANE)
            a0 = j * HI + h
            into = [None] * (tiles + 1)
            denom = row_ref[a0]

            def put(t):
                a, b = t * LANE, min((t + 1) * LANE, vir)
                value = into[t][:, : b - a] / (denom - vir_ref[:, a:b])
                done[a0, :, a:b] += value

            for w in range(count):
                seg = got[w, rows, src * LANE : (src + 1) * LANE].astype(F32)
                if off + width > LANE:
                    nxt = got[w, rows, (src + 1) * LANE : (src + 2) * LANE].astype(F32)
                    seg = jnp.where(lane >= off, seg, nxt)
                to, at = divmod(w * width, LANE)
                shift = (at - off) % LANE
                if shift:
                    seg = pltpu.roll(seg, shift, 1)
                into[to] = seg if into[to] is None else jnp.where(lane >= at, seg, into[to])
                if at + width > LANE:
                    into[to + 1] = seg
                if at + width >= LANE or w == count - 1:
                    put(to)
                if at + width > LANE and w == count - 1:
                    put(to + 1)
        leave(j).start()
        return carry

    lax.fori_loop(0, blocks, block, 0)
    for j in range(blocks):
        leave(j).wait()


def finish(got, rowterm, vir_row, base, skip, rows):
    width, pairs, vir = base.shape
    return pl.pallas_call(
        functools.partial(finish_kernel, width, skip),
        in_specs=[HBM, HBM, VMEM, HBM],
        out_specs=HBM,
        out_shape=pltpu.HBM((width, pairs, vir), F32),
        input_output_aliases={3: 0},
        scratch_shapes=[
            pltpu.VMEM(got.shape, BF),
            pltpu.VMEM((rows, pairs, vir), F32),
            pltpu.VMEM((rows, pairs, 1), F32),
            pltpu.SemaphoreType.DMA((rows // HI,)),
            pltpu.SemaphoreType.DMA((2, rows // HI)),
            pltpu.SemaphoreType.DMA,
        ],
        compiler_params=params(16),
        cost_estimate=cost(1e8, 16e6),
        name="left_add",
    )(got, in_hbm(rowterm), vir_row, in_hbm(base))


def per_device(amplitudes, integrals, fock_vv, eps_occ, eps_vir, pair_ids, mirror_row):
    pairs, width, vir = amplitudes.shape
    count = lax.axis_size("vir")
    own = amplitudes.transpose(1, 0, 2)
    blocks = lax.axis_size("occ")
    other = lax.ppermute(own, "occ", [(i, i ^ 1) for i in range(blocks)])

    call = functools.partial(wire_call, count=count, width=width, pairs=pairs, vir=vir)
    rows_one, mine = fprep(fock_vv, count, 0, own)
    args = (mirror_row, mine, in_hbm(other), rows_one)
    specs = [SMEM, VMEM, HBM, VMEM]
    sent_one, x = call(lead_kernel, "left_lead", True, args, specs, lo_count=LO[0])
    sent_one, eps_occ, eps_vir, pair_ids, mirror = lax.optimization_barrier(
        (sent_one, eps_occ, eps_vir, pair_ids, mirror_row)
    )
    got_one = lax.all_to_all(sent_one, "vir", 0, 0, tiled=True)

    occ = jnp.arange(eps_occ.shape[0], dtype=jnp.int32)
    first = jnp.sum(jnp.where(pair_ids[:, 0:1] == occ[None, :], eps_occ[None, :], 0.0), axis=1)
    second = jnp.sum(jnp.where(pair_ids[:, 1:2] == occ[None, :], eps_occ[None, :], 0.0), axis=1)
    local = lax.dynamic_slice_in_dim(eps_vir, lax.axis_index("vir") * width, width)
    rowterm = ((first + second)[None, :] - local[:, None])[:, :, None]
    vir_row = eps_vir[None, :]

    (rows_two,) = fprep(fock_vv, count, 1)
    args = (rows_two, in_hbm(x))
    (sent_two,) = call(send_kernel, "left_send", False, args, [VMEM, HBM], lo_count=LO[1])
    got_two = lax.all_to_all(sent_two, "vir", 0, 0, tiled=True)
    ints = integrals.transpose(1, 0, 2)
    part, cut = 15, LO[0] * HI
    source = jnp.arange(part, dtype=jnp.int32)[:, None] * pairs + mirror[None, :]
    swap = (source.reshape(-1, 1) == jnp.arange(part * pairs, dtype=jnp.int32)).astype(BF)
    base = right(swap, own, other, ints, fock_vv, rowterm, vir_row, part)
    out = finish(got_one, rowterm, vir_row, base, 0, cut)
    out = finish(got_two, rowterm, vir_row, out, cut, width - cut)
    return out.transpose(1, 0, 2)


def solution(mesh):
    return jax.shard_map(
        per_device,
        mesh=mesh,
        in_specs=(
            P("occ", "vir", None),
            P("occ", "vir", None),
            P(),
            P(),
            P(),
            P("occ", None),
            P("occ"),
        ),
        out_specs=P("occ", "vir", None),
        check_vma=False,
    )
```

```python
import functools

import jax
import jax.numpy as jnp
from jax import lax
from jax.experimental import pallas as pl
from jax.experimental.pallas import tpu as pltpu
from jax.sharding import PartitionSpec as P

BF = jnp.bfloat16
F32 = jnp.float32
LANE = 128
HI = 5
LO = (8, 7)
STEP_V = 8
ROWS = STEP_V * HI * 8
HBM = pl.BlockSpec(memory_space=pltpu.HBM)
VMEM = pl.BlockSpec(memory_space=pltpu.VMEM)
SMEM = pl.BlockSpec(memory_space=pltpu.SMEM)


def nt(a, b):
    return lax.dot_general(a, b, (((1,), (1,)), ((), ())), preferred_element_type=F32)


def params(mib):
    return pltpu.CompilerParams(vmem_limit_bytes=mib << 20)


def cost(flops, moved):
    return pl.CostEstimate(flops=int(flops), bytes_accessed=int(moved), transcendentals=0)


def resident(x):
    return pltpu.with_memory_space_constraint(x, pltpu.VMEM)


def in_hbm(x):
    return pltpu.with_memory_space_constraint(x, pltpu.HBM)


def reorder(pairs, size, mirror_ref=None):
    row = lax.broadcasted_iota(jnp.int32, (16 * pairs, 1), 0)
    pair, at = row // 16, row % 16
    source = pair if mirror_ref is None else mapped(pair, pairs, mirror_ref)
    col = lax.broadcasted_iota(jnp.int32, (1, size * pairs), 1)
    return (at * pairs + source == col).astype(F32).astype(BF)


def mapped(pair, pairs, mirror_ref):
    out = jnp.zeros_like(pair)
    for p in range(pairs):
        out = jnp.where(pair == p, mirror_ref[p], out)
    return out


def pick_rows(width, chunk, g, window, low, high):
    row = lax.broadcasted_iota(jnp.int32, (ROWS, 1), 0)
    dest, hi, lo = row // (HI * 8), (row // 8) % HI, row % 8
    base = sum(LO[:chunk]) * HI
    source = jnp.where(lo < LO[chunk], dest * width + base + lo * HI + hi, -1000)
    col = lax.broadcasted_iota(jnp.int32, (1, high - low), 1) + (low - g * STEP_V * width)
    hot = (source == col).astype(F32).astype(BF)
    return jnp.dot(hot, window, preferred_element_type=F32).astype(BF)


def fprep_kernel(width, chunk, f_ref, *rest):
    moved = chunk == 0
    if moved:
        own_ref, out_ref, mine_ref, f_vmem, sems, own, own_sems = rest
    else:
        out_ref, f_vmem, sems = rest
    groups = f_ref.shape[0] // width // STEP_V
    span = STEP_V * width
    lows = [g * span // 16 * 16 for g in range(groups)]
    highs = [-(-(g + 1) * span // 16) * 16 for g in range(groups)]
    cuts = [0] + highs
    copies, own_copies = [], []
    for g in range(groups):
        part = pl.ds(cuts[g], cuts[g + 1] - cuts[g])
        copies.append(pltpu.make_async_copy(f_ref.at[part], f_vmem.at[part], sems.at[g]))
        copies[-1].start()
    if moved:
        for j in range(0, width, 16):
            part = pl.ds(j, min(16, width - j))
            own_copies.append(pltpu.make_async_copy(own_ref.at[part], own.at[part], own_sems.at[j // 16]))
            own_copies[-1].start()
    for g in range(groups):
        copies[g].wait()
        window = f_vmem[lows[g] : highs[g], :]
        picked = pick_rows(width, chunk, g, window, lows[g], highs[g])
        out_ref[g * ROWS : (g + 1) * ROWS, :] = picked
    if moved:
        pairs, vir = own.shape[1], own.shape[2]
        move = reorder(pairs, 16)
        for j in range(0, width, 16):
            size = min(16, width - j)
            own_copies[j // 16].wait()
            mine = own[j : j + size].reshape(size * pairs, vir)
            mine = jnp.dot(move[:, : size * pairs], mine, preferred_element_type=F32)
            mine_ref[:, j : j + 16, :] = mine.astype(BF).reshape(pairs, 16, vir)


def fprep(fock, count, chunk, own=None):
    vir = fock.shape[0]
    groups = count // STEP_V
    out_shape = [pltpu.VMEM((count * HI * 8, vir), BF)]
    scratch = [pltpu.VMEM((vir, vir), BF), pltpu.SemaphoreType.DMA((groups,))]
    args = [in_hbm(fock)]
    if own is not None:
        width, pairs, _ = own.shape
        blocks = -(-width // 16)
        out_shape.append(pltpu.VMEM((pairs, 16 * blocks, vir), BF))
        scratch += [pltpu.VMEM(own.shape, BF), pltpu.SemaphoreType.DMA((blocks,))]
        args.append(in_hbm(own))
    return pl.pallas_call(
        functools.partial(fprep_kernel, vir // count, chunk),
        in_specs=[HBM] * len(args),
        out_specs=[VMEM] * len(out_shape),
        out_shape=out_shape,
        scratch_shapes=scratch,
        compiler_params=params(30 if own is None else 48),
        cost_estimate=cost(4e9, 18e6),
        name="fock_rows",
    )(*args)


def product_straight(width, lo_count, f_ref, x_ref, out_ref, acc0, acc1, stage, wire, sems):
    pairs, pitch, vir = x_ref.shape
    flat = x_ref.reshape(pairs * pitch, vir)
    groups = f_ref.shape[0] // ROWS
    tiles = pairs * pitch // 256
    accs = (acc0, acc1)
    copies = []
    for g in range(groups + 1):
        for n in range(tiles):
            if g < groups:
                accs[g % 2][:, n * 256 : (n + 1) * 256] = nt(
                    f_ref[g * ROWS : (g + 1) * ROWS, :], flat[n * 256 : (n + 1) * 256, :]
                )
            for v in range(n * STEP_V // tiles, (n + 1) * STEP_V // tiles):
                if g > 0:
                    acc = accs[(g + 1) % 2]
                    at = (g - 1) * STEP_V + v
                    pack(width, pairs, pitch, lo_count, acc, v * HI * 8, stage.at[v % 2], wire, at)
        if g > 0:
            part = pl.ds((g - 1) * STEP_V, STEP_V)
            copies.append(pltpu.make_async_copy(wire.at[part], out_ref.at[part], sems.at[g - 1]))
            copies[-1].start()
    for copy in copies:
        copy.wait()


def product(width, lo_count, f_ref, x_ref, out_ref, acc0, acc1, stage, wire, sems):
    pairs, pitch, vir = x_ref.shape
    flat = x_ref.reshape(pairs * pitch, vir)
    groups = f_ref.shape[0] // ROWS
    tiles = pairs * pitch // 256
    accs = (acc0, acc1)

    def multiply(g, n):
        lanes = pl.ds(pl.multiple_of(n * 256, 256), 256)
        accs[g % 2][:, lanes] = nt(f_ref[g * ROWS : (g + 1) * ROWS, :], flat[lanes, :])

    def packed(g, v, slot):
        row = pl.multiple_of(v * (HI * 8), 8)
        pack(width, pairs, pitch, lo_count, accs[g % 2], row, stage.at[slot], wire, g * STEP_V + v)

    def leave(g):
        part = pl.ds(g * STEP_V, STEP_V)
        return pltpu.make_async_copy(wire.at[part], out_ref.at[part], sems.at[g])

    for g in range(groups):

        def step(n, carry, g=g):
            multiply(g, n)
            if g > 0:
                packed(g - 1, n, 0)
                packed(g - 1, jnp.minimum(tiles + n, STEP_V - 1), 1)
            return carry

        lax.fori_loop(0, tiles, step, 0)
        if g > 0:
            leave(g - 1).start()

    def last(n, carry):
        packed(groups - 1, 2 * n, 0)
        packed(groups - 1, 2 * n + 1, 1)
        return carry

    lax.fori_loop(0, STEP_V // 2, last, 0)
    leave(groups - 1).start()
    for g in range(groups):
        leave(g).wait()


def pack(width, pairs, pitch, lo_count, acc_ref, row, stage_ref, wire_ref, v):
    lane = lax.broadcasted_iota(jnp.int32, (8, LANE), 1)
    tiles = wire_ref.shape[2] // LANE
    for p in range(pairs):
        tile, off = divmod(p * pitch, LANE)
        into = [None] * tiles
        for h in range(HI):
            rows = pl.ds(pl.multiple_of(row + 8 * h, 8), 8)
            seg = acc_ref[rows, tile * LANE : (tile + 1) * LANE]
            if off + width > LANE:
                nxt = acc_ref[rows, (tile + 1) * LANE : (tile + 2) * LANE]
                seg = jnp.where(lane >= off, seg, nxt)
            to, at = divmod(h * width, LANE)
            shift = (at - off) % LANE
            if shift:
                seg = pltpu.roll(seg, shift, 1)
            into[to] = seg if into[to] is None else jnp.where(lane >= at, seg, into[to])
            if at + width > LANE:
                into[to + 1] = seg
        for t in range(tiles):
            stage_ref[t, pl.ds(p, 8, stride=pairs), :] = into[t]
    for t in range(tiles):
        block = stage_ref[t, : lo_count * pairs, :].astype(BF)
        wire_ref[v, :, t * LANE : (t + 1) * LANE] = block


def lead_kernel(
    width, lo_count, mirror_ref, mine_ref, other_ref, f_ref, out_ref, x_ref, x2, sems, other, *scratch
):
    pairs, vir = other.shape[1], other.shape[2]
    starts = range(0, width, 16)
    ins = []
    for j in starts:
        part = pl.ds(j, min(16, width - j))
        ins.append(pltpu.make_async_copy(other_ref.at[part], other.at[part], sems.at[0, j // 16]))
        ins[-1].start()
    outs = []
    pick = reorder(pairs, 16, mirror_ref)
    for j in starts:
        size = min(16, width - j)
        ins[j // 16].wait()
        theirs = other[j : j + size].reshape(size * pairs, vir)
        theirs = jnp.dot(pick[:, : size * pairs], theirs, preferred_element_type=F32).reshape(pairs, 16, vir)
        mine = mine_ref[:, j : j + 16, :].astype(F32)
        x2[:, j : j + 16, :] = (2.0 * theirs - mine).astype(BF)
        part = pl.ds(j, 16)
        outs.append(pltpu.make_async_copy(x2.at[:, part], x_ref.at[:, part], sems.at[1, j // 16]))
        outs[-1].start()
    product_straight(width, lo_count, f_ref, x2, out_ref, *scratch)
    for copy in outs:
        copy.wait()


def send_kernel(width, lo_count, f_ref, x_ref, out_ref, x2, sems, *scratch):
    copy = pltpu.make_async_copy(x_ref, x2, sems.at[0, 0])
    copy.start()
    copy.wait()
    product(width, lo_count, f_ref, x2, out_ref, *scratch)


def wire_call(kernel, name, x_out, args, specs, count, width, pairs, lo_count, vir):
    pitch = -(-width // 16) * 16
    wide = -(-HI * width // LANE) * LANE
    wire = (count, lo_count * pairs, wide)
    out_shape = [pltpu.HBM(wire, BF)]
    out_specs = [HBM]
    blocks = pitch // 16
    scratch = [pltpu.VMEM((pairs, pitch, vir), BF), pltpu.SemaphoreType.DMA((2, blocks))]
    if x_out:
        out_shape.append(pltpu.HBM((pairs, pitch, vir), BF))
        out_specs.append(HBM)
        scratch.append(pltpu.VMEM((width, pairs, vir), BF))
    return pl.pallas_call(
        functools.partial(kernel, width, lo_count),
        in_specs=specs,
        out_specs=out_specs,
        out_shape=out_shape,
        scratch_shapes=scratch
        + [
            pltpu.VMEM((ROWS, pairs * pitch), F32),
            pltpu.VMEM((ROWS, pairs * pitch), F32),
            pltpu.VMEM((2, wide // LANE, 8 * pairs, LANE), F32),
            pltpu.VMEM(wire, BF),
            pltpu.SemaphoreType.DMA((count // STEP_V,)),
        ],
        compiler_params=params(28),
        cost_estimate=cost(2.0 * count * HI * 8 * pairs * pitch * vir, 10e6),
        name=name,
    )(*args)


def right_kernel(swap_ref, own_ref, other_ref, int_ref, f_ref, row_ref, vir_ref, out_ref):
    part, pairs, vir = own_ref.shape
    rows = part * pairs
    own = own_ref[...].reshape(rows, vir)
    other = other_ref[...].reshape(rows, vir)
    theirs = jnp.dot(swap_ref[...], other, preferred_element_type=F32)
    tilde = (2.0 * own.astype(F32) - theirs).astype(BF)
    for n in range(0, vir, 512):
        m = min(n + 512, vir)
        right = nt(tilde, f_ref[n:m, :]).astype(BF).astype(F32)
        denom = row_ref[...].reshape(rows, 1) - vir_ref[:, n:m]
        total = int_ref[:, :, n:m].reshape(rows, m - n).astype(F32) + right
        res = own_ref[:, :, n:m].reshape(rows, m - n).astype(F32) + total / denom
        out_ref[:, :, n:m] = res.reshape(part, pairs, m - n)


def right(swap, own, other, integrals, fock, rowterm, vir_row, part=15):
    width, pairs, vir = own.shape
    block = pl.BlockSpec((part, pairs, vir), lambda j: (j, 0, 0))
    return pl.pallas_call(
        right_kernel,
        grid=(width // part,),
        in_specs=[
            pl.BlockSpec((part * pairs, part * pairs), lambda j: (0, 0)),
            block,
            block,
            block,
            pl.BlockSpec((vir, vir), lambda j: (0, 0), pipeline_mode=pl.Buffered(1)),
            pl.BlockSpec((part, pairs, 1), lambda j: (j, 0, 0)),
            pl.BlockSpec((1, vir), lambda j: (0, 0)),
        ],
        out_specs=block,
        out_shape=jax.ShapeDtypeStruct((width, pairs, vir), F32),
        compiler_params=params(36),
        cost_estimate=cost(2.0 * width * pairs * vir * vir, 40e6),
        name="right_term",
    )(swap, in_hbm(own), in_hbm(other), in_hbm(integrals), in_hbm(fock), rowterm, vir_row)


def finish_kernel(
    width, skip, got_ref, row_hbm, vir_ref, base_ref, out_ref, got, done, row_ref, sems, got_sems, row_sem
):
    row_copy = pltpu.make_async_copy(row_hbm.at[pl.ds(skip, done.shape[0])], row_ref, row_sem)
    row_copy.start()
    count = got.shape[0]
    pairs, vir = base_ref.shape[1], base_ref.shape[2]
    lane = lax.broadcasted_iota(jnp.int32, (pairs, LANE), 1)
    tiles = -(-vir // LANE)
    blocks = done.shape[0] // HI

    def arrivals(j):
        rows = pl.ds(pl.multiple_of(j * pairs, 16), pairs)
        part, where = pl.ds(j * HI, HI), pl.ds(skip + j * HI, HI)
        return (
            pltpu.make_async_copy(got_ref.at[:, rows], got.at[:, rows], got_sems.at[0, j]),
            pltpu.make_async_copy(base_ref.at[where], done.at[part], got_sems.at[1, j]),
        )

    def leave(j):
        part, where = pl.ds(j * HI, HI), pl.ds(skip + j * HI, HI)
        return pltpu.make_async_copy(done.at[part], out_ref.at[where], sems.at[j])

    for j in range(blocks):
        for copy in arrivals(j):
            copy.start()
    row_copy.wait()

    def block(j, carry):
        for copy in arrivals(j):
            copy.wait()
        rows = pl.ds(pl.multiple_of(j * pairs, 16), pairs)
        for h in range(HI):
            src, off = divmod(h * width, LANE)
            a0 = j * HI + h
            into = [None] * (tiles + 1)
            denom = row_ref[a0]

            def put(t):
                a, b = t * LANE, min((t + 1) * LANE, vir)
                value = into[t][:, : b - a] / (denom - vir_ref[:, a:b])
                done[a0, :, a:b] += value

            for w in range(count):
                seg = got[w, rows, src * LANE : (src + 1) * LANE].astype(F32)
                if off + width > LANE:
                    nxt = got[w, rows, (src + 1) * LANE : (src + 2) * LANE].astype(F32)
                    seg = jnp.where(lane >= off, seg, nxt)
                to, at = divmod(w * width, LANE)
                shift = (at - off) % LANE
                if shift:
                    seg = pltpu.roll(seg, shift, 1)
                into[to] = seg if into[to] is None else jnp.where(lane >= at, seg, into[to])
                if at + width > LANE:
                    into[to + 1] = seg
                if at + width >= LANE or w == count - 1:
                    put(to)
                if at + width > LANE and w == count - 1:
                    put(to + 1)
        leave(j).start()
        return carry

    lax.fori_loop(0, blocks, block, 0)
    for j in range(blocks):
        leave(j).wait()


def finish(got, rowterm, vir_row, base, skip, rows):
    width, pairs, vir = base.shape
    return pl.pallas_call(
        functools.partial(finish_kernel, width, skip),
        in_specs=[HBM, HBM, VMEM, HBM],
        out_specs=HBM,
        out_shape=pltpu.HBM((width, pairs, vir), F32),
        input_output_aliases={3: 0},
        scratch_shapes=[
            pltpu.VMEM(got.shape, BF),
            pltpu.VMEM((rows, pairs, vir), F32),
            pltpu.VMEM((rows, pairs, 1), F32),
            pltpu.SemaphoreType.DMA((rows // HI,)),
            pltpu.SemaphoreType.DMA((2, rows // HI)),
            pltpu.SemaphoreType.DMA,
        ],
        compiler_params=params(16),
        cost_estimate=cost(1e8, 16e6),
        name="left_add",
    )(got, in_hbm(rowterm), vir_row, in_hbm(base))


def per_device(amplitudes, integrals, fock_vv, eps_occ, eps_vir, pair_ids, mirror_row):
    pairs, width, vir = amplitudes.shape
    count = lax.axis_size("vir")
    own = amplitudes.transpose(1, 0, 2)
    blocks = lax.axis_size("occ")
    other = lax.ppermute(own, "occ", [(i, i ^ 1) for i in range(blocks)])

    call = functools.partial(wire_call, count=count, width=width, pairs=pairs, vir=vir)
    rows_one, mine = fprep(fock_vv, count, 0, own)
    args = (mirror_row, mine, in_hbm(other), rows_one)
    specs = [SMEM, VMEM, HBM, VMEM]
    sent_one, x = call(lead_kernel, "left_lead", True, args, specs, lo_count=LO[0])
    sent_one, eps_occ, eps_vir, pair_ids, mirror = lax.optimization_barrier(
        (sent_one, eps_occ, eps_vir, pair_ids, mirror_row)
    )
    got_one = lax.all_to_all(sent_one, "vir", 0, 0, tiled=True)

    occ = jnp.arange(eps_occ.shape[0], dtype=jnp.int32)
    first = jnp.sum(jnp.where(pair_ids[:, 0:1] == occ[None, :], eps_occ[None, :], 0.0), axis=1)
    second = jnp.sum(jnp.where(pair_ids[:, 1:2] == occ[None, :], eps_occ[None, :], 0.0), axis=1)
    local = lax.dynamic_slice_in_dim(eps_vir, lax.axis_index("vir") * width, width)
    rowterm = ((first + second)[None, :] - local[:, None])[:, :, None]
    vir_row = eps_vir[None, :]

    (rows_two,) = fprep(fock_vv, count, 1)
    args = (rows_two, in_hbm(x))
    (sent_two,) = call(send_kernel, "left_send", False, args, [VMEM, HBM], lo_count=LO[1])
    got_two = lax.all_to_all(sent_two, "vir", 0, 0, tiled=True)
    ints = integrals.transpose(1, 0, 2)
    part, cut = 15, LO[0] * HI
    source = jnp.arange(part, dtype=jnp.int32)[:, None] * pairs + mirror[None, :]
    swap = (source.reshape(-1, 1) == jnp.arange(part * pairs, dtype=jnp.int32)).astype(BF)
    base = right(swap, own, other, ints, fock_vv, rowterm, vir_row, part)
    out = finish(got_one, rowterm, vir_row, base, 0, cut)
    out = finish(got_two, rowterm, vir_row, out, cut, width - cut)
    return out.transpose(1, 0, 2)


def solution(mesh):
    return jax.shard_map(
        per_device,
        mesh=mesh,
        in_specs=(
            P("occ", "vir", None),
            P("occ", "vir", None),
            P(),
            P(),
            P(),
            P("occ", None),
            P("occ"),
        ),
        out_specs=P("occ", "vir", None),
        check_vma=False,
    )
```
